128 devices in a mesh: replica: 8 (over x, y_hi), shard: 16 (over z, y_lo, core).
Axes of the slice: x: 4, y: 4 (y_hi: 2, y_lo: 2; y = y_hi * 2 + y_lo), z: 4, core: 2. Of those that a mesh axis runs over, the one named last changes fastest.
Arguments:
- tokens: bfloat16 [65536, 1920], P(('replica', 'shard')), may hold values from -36 to 36
- timesteps: int32 [256], P(('replica', 'shard')), may hold values from 0 to 63
- table: float32 [64, 2, 1920], replicated, may hold values from -3 to 3
- weight_values: bfloat16 [4864, 1920], P('shard'), may hold values from -0.125 to 0.125
- weight_scales: bfloat16 [4864, 15], P('shard'), may hold values from 0.29882812 to 3
- cotangent: bfloat16 [65536, 4864], P(('replica', 'shard')), may hold values from -24 to 24
Outputs:
- hidden: bfloat16 [65536, 4864], P(('replica', 'shard'))
- grad_weight: float32 [4864, 1920], P('shard')
- grad_tokens: bfloat16 [65536, 1920], P(('replica', 'shard'))
The draws below stay inside these ranges and needn't reach their ends.
All inputs are finite; a program needn't handle non-finite values.
Results may differ from the reference program's by a relative error of at most 0.02.
Values may be sent and summed in bfloat16 or wider, within the bound.
A program may use at most 256 MiB of HBM per device.

```python
import math
import jax
import jax.numpy as jnp
from jax import lax

D = 1920
FFW = 4864
QBLOCK = 128
NSTEPS = 64
TOK_DEV = 512
SAMPLES = 256
TOKENS = 65536
N_REPLICA = 8
N_SHARD = 16


def draw_tokens(key, part):
    subkeys = jax.random.split(jax.random.fold_in(key, 11), 3)
    row_scale = jnp.exp(jax.random.uniform(subkeys[0], (TOKENS, 1), jnp.float32, math.log(0.3), math.log(3.0)))
    column_scale = jnp.exp(jax.random.uniform(subkeys[1], (1, D), jnp.float32, math.log(0.3), math.log(3.0)))
    noise_core = jax.random.truncated_normal(subkeys[2], -4.0, 4.0, (TOKENS, D), jnp.float32)
    drawn = noise_core * column_scale * row_scale
    return drawn.astype(jnp.bfloat16)


def touch_ends(values, rng, least, top_value):
    index_at = [jax.random.randint(jax.random.fold_in(rng, axis), (), 0, length) for axis, length in enumerate(values.shape)]
    longest = values.shape.index(max(values.shape))
    next_to = index_at[:longest] + [(index_at[longest] + 1) % values.shape[longest]] + index_at[longest + 1:]
    return values.at[tuple(index_at)].set(least).at[tuple(next_to)].set(top_value)


def strengthened(values, own_key, source, target, shards_of, factor):
    owner, partner = [(jnp.arange(values.shape[axis_at]) // (values.shape[axis_at] // shards_of)).reshape([-1 if axis == axis_at else 1 for axis in range(values.ndim)]) for axis_at in (source, target)]
    chosen = jax.random.permutation(own_key, shards_of)[partner]
    strong = (owner == chosen) | (owner == (partner + shards_of // 2) % shards_of)
    return jnp.where(strong, factor * values, values)


def block_levels(rng, shape, shards, least, top_value):
    def one(axis_at, shards_of):
        steps = jax.random.uniform(jax.random.fold_in(jax.random.fold_in(rng, 6), axis_at), (shards_of,), jnp.float32, least / len(shards), top_value / len(shards))
        return jnp.repeat(jnp.exp(steps), shape[axis_at] // shards_of).reshape((-1,) + (1,) * (len(shape) - axis_at - 1))

    loudness = one(*shards[0])
    for cut in shards[1:]:
        loudness = loudness * one(*cut)
    return loudness


def scatter_about(stream_key, extent, scale, most, shards=(), kind=jnp.bfloat16):
    values = jax.random.normal(stream_key, extent, jnp.float32) * scale
    if len(shards) > 0:
        values = block_levels(stream_key, extent, shards, -0.22, 0.18) * values
    return jnp.clip(values, min=-most, max=most).astype(kind)


def gaussian_with(stream_key, extent, width, limit, shards, heavy, kind=jnp.bfloat16):
    values = width * jax.random.normal(stream_key, extent, jnp.float32)
    if shards:
        values = values * block_levels(stream_key, extent, shards, -0.22, 0.18)
    return jnp.clip(strengthened(values, jax.random.fold_in(stream_key, 3), *heavy), -limit, limit).astype(kind)


def setup_inputs(seed: int = 0) -> dict:
    key_of = jax.random.split(jax.random.key(seed), 7)
    return {
        "tokens": draw_tokens(jax.random.fold_in(key_of[6], 71), 0),
        "timesteps": touch_ends(jax.random.randint(key_of[1], (SAMPLES,), 0, NSTEPS), jax.random.fold_in(key_of[1], 1), 0, NSTEPS - 1).astype(jnp.int32),
        "table": scatter_about(key_of[2], (NSTEPS, 2, D), 0.5, 3.0, (), jnp.float32),
        "weight_values": scatter_about(key_of[3], (FFW, D), D ** -0.5, 0.125, ((0, 16),)),
        "weight_scales": jnp.clip(jnp.exp(math.log(3.0) - 2.306499 * jax.random.uniform(key_of[4], (FFW, D // QBLOCK), jnp.float32) ** block_levels(key_of[4], (FFW, D // QBLOCK), ((0, 16),), -0.2, 0.2)), 0.29882812, 3.0).astype(jnp.bfloat16),
        "cotangent": gaussian_with(key_of[5], (TOKENS, FFW), 1.0, 24.0, ((0, 128),), (0, 1, 128, 5.5)),
    }


root_two_over_pi = 0.7978845608028654
cubic_coef = 0.044715
epsilon = 1e-06

def gelu_slope(preact):
    inner_term = root_two_over_pi * (preact + cubic_coef * preact * preact * preact)
    tangent = jnp.tanh(inner_term)
    gelu_value = 0.5 * preact * (1.0 + tangent)
    derivative = 0.5 * (1.0 + tangent) + 0.5 * preact * (1.0 - tangent * tangent) * root_two_over_pi * (1.0 + 3.0 * cubic_coef * preact * preact)
    return (gelu_value, derivative)

def dequantize(weight_values, weight_scales):
    row_count, features = weight_values.shape
    blocks = weight_scales.shape[1]
    expanded = weight_values.astype(jnp.float32).reshape(row_count, blocks, features // blocks) * weight_scales.astype(jnp.float32)[:, :, None]
    return expanded.reshape(row_count, features).astype(jnp.bfloat16)

def modulate(tokens, timesteps, table):
    samples = timesteps.shape[0]
    step_count = table.shape[0]
    features = tokens.shape[1]
    onehot = (timesteps[:, None] == jnp.arange(step_count, dtype=jnp.int32)[None, :]).astype(jnp.float32)
    picked = jnp.dot(onehot, table.reshape(step_count, 2 * features), precision=lax.Precision.HIGHEST)
    picked = picked.reshape(samples, 2, features)
    grouped = tokens.astype(jnp.float32).reshape(samples, -1, features)
    centre = grouped - lax.optimization_barrier(jnp.mean(grouped, axis=2, keepdims=True))
    inverse = lax.rsqrt(lax.optimization_barrier(jnp.mean(centre * centre, axis=2, keepdims=True)) + epsilon)
    normed = centre * inverse
    factor = 1.0 + picked[:, 1][:, None, :]
    moved = (normed * factor + picked[:, 0][:, None, :]).reshape(-1, features).astype(jnp.bfloat16)
    return (moved, normed, inverse, factor)

def normalize_back(grad_moved, normed, inverse, factor):
    samples = normed.shape[0]
    features = normed.shape[2]
    scaled_grad = grad_moved.reshape(samples, -1, features) * factor
    mean_grad = lax.optimization_barrier(jnp.mean(scaled_grad, axis=2, keepdims=True))
    mean_prod = lax.optimization_barrier(jnp.mean(scaled_grad * normed, axis=2, keepdims=True))
    result = inverse * (scaled_grad - mean_grad - normed * mean_prod)
    return result.reshape(-1, features).astype(jnp.bfloat16)

def reference(tokens, timesteps, table, weight_values, weight_scales, cotangent):
    moved, normed, inverse, factor = modulate(tokens, timesteps, table)
    weight = dequantize(weight_values, weight_scales)
    weight_wide = weight.astype(jnp.float32)
    moved_wide = moved.astype(jnp.float32)
    preact = jnp.dot(moved_wide, weight_wide.T, precision=lax.Precision.HIGHEST)
    gelu_value, derivative = gelu_slope(preact)
    hidden = gelu_value.astype(jnp.bfloat16)
    grad_pre = (cotangent.astype(jnp.float32) * derivative).astype(jnp.bfloat16)
    grad_pre_wide = grad_pre.astype(jnp.float32)
    grad_moved = jnp.dot(grad_pre_wide, weight_wide, precision=lax.Precision.HIGHEST)
    grad_tokens = normalize_back(grad_moved, normed, inverse, factor)
    devices = N_REPLICA * N_SHARD
    grad_blocks = grad_pre_wide.reshape(devices, TOK_DEV, grad_pre.shape[1])
    moved_blocks = moved_wide.reshape(devices, TOK_DEV, moved.shape[1])

    def accumulate(running, blocks_pair):
        grad_term = jnp.dot(blocks_pair[0].T, blocks_pair[1], precision=lax.Precision.HIGHEST)
        rounded = lax.optimization_barrier(grad_term.astype(jnp.bfloat16))
        return (running + rounded.astype(jnp.float32), None)
    initial = jnp.zeros((grad_pre.shape[1], moved.shape[1]), jnp.float32)
    grad_weight, _ = lax.scan(accumulate, initial, (grad_blocks, moved_blocks))
    return (hidden, grad_weight, grad_tokens)
```

```python
import jax
import jax.numpy as jnp
from jax import lax
from jax.sharding import PartitionSpec as P

root_two_over_pi = 0.7978845608028654
cubic_coef = 0.044715
epsilon = 1e-06


def gelu_slope(preact):
    inner_term = root_two_over_pi * (preact + cubic_coef * preact * preact * preact)
    tangent = jnp.tanh(inner_term)
    gelu_value = 0.5 * preact * (1.0 + tangent)
    derivative = 0.5 * (1.0 + tangent) + 0.5 * preact * (
        1.0 - tangent * tangent
    ) * root_two_over_pi * (1.0 + 3.0 * cubic_coef * preact * preact)
    return (gelu_value, derivative)


def dequantize(weight_values, weight_scales):
    row_count, features = weight_values.shape
    blocks = weight_scales.shape[1]
    expanded = (
        weight_values.astype(jnp.float32).reshape(row_count, blocks, features // blocks)
        * weight_scales.astype(jnp.float32)[:, :, None]
    )
    return expanded.reshape(row_count, features).astype(jnp.bfloat16)


def modulate(tokens, timesteps, table):
    samples = timesteps.shape[0]
    step_count = table.shape[0]
    features = tokens.shape[1]
    onehot = (timesteps[:, None] == jnp.arange(step_count, dtype=jnp.int32)[None, :]).astype(
        jnp.float32
    )
    picked = jnp.dot(
        onehot, table.reshape(step_count, 2 * features), precision=lax.Precision.HIGHEST
    )
    picked = picked.reshape(samples, 2, features)
    grouped = tokens.astype(jnp.float32).reshape(samples, -1, features)
    centre = grouped - jnp.mean(grouped, axis=2, keepdims=True)
    inverse = lax.rsqrt(jnp.mean(centre * centre, axis=2, keepdims=True) + epsilon)
    normed = centre * inverse
    factor = 1.0 + picked[:, 1][:, None, :]
    moved = (normed * factor + picked[:, 0][:, None, :]).reshape(-1, features).astype(jnp.bfloat16)
    return (moved, normed, inverse, factor)


def normalize_back(grad_moved, normed, inverse, factor):
    samples = normed.shape[0]
    features = normed.shape[2]
    scaled_grad = grad_moved.reshape(samples, -1, features) * factor
    mean_grad = jnp.mean(scaled_grad, axis=2, keepdims=True)
    mean_prod = jnp.mean(scaled_grad * normed, axis=2, keepdims=True)
    result = inverse * (scaled_grad - mean_grad - normed * mean_prod)
    return result.reshape(-1, features).astype(jnp.bfloat16)


def per_device(tokens, timesteps, table, weight_values, weight_scales, cotangent):
    moved, normed, inverse, factor = modulate(tokens, timesteps, table)
    upstream = cotangent.astype(jnp.float32)
    weight = lax.all_gather(
        dequantize(weight_values, weight_scales), "shard", axis=0, tiled=True
    )
    preact = jnp.einsum("td,fd->tf", moved, weight, preferred_element_type=jnp.float32)
    gelu_value, derivative = gelu_slope(preact)
    hidden = gelu_value.astype(jnp.bfloat16)
    grad_pre = (upstream * derivative).astype(jnp.bfloat16)
    grad_moved = jnp.dot(grad_pre, weight, preferred_element_type=jnp.float32)
    product = lax.dot_general(
        grad_pre, moved, (((0,), (0,)), ((), ())), preferred_element_type=jnp.float32
    )
    rounded = lax.optimization_barrier(product.astype(jnp.bfloat16))
    group_part = lax.psum_scatter(
        rounded.astype(jnp.float32).astype(jnp.bfloat16), "shard", scatter_dimension=0, tiled=True
    )
    grad_weight = lax.psum(group_part, "replica").astype(jnp.float32)
    grad_tokens = normalize_back(grad_moved, normed, inverse, factor)
    return (hidden, grad_weight, grad_tokens)


def solution(mesh):
    placed = (
        P(("replica", "shard"), None),
        P(("replica", "shard")),
        P(),
        P("shard", None),
        P("shard", None),
        P(("replica", "shard"), None),
    )
    return jax.shard_map(
        per_device,
        mesh=mesh,
        in_specs=placed,
        out_specs=(P(("replica", "shard"), None), P("shard", None), P(("replica", "shard"), None)),
        check_vma=False,
    )
```

```python
import jax
import jax.numpy as jnp
from jax import lax
from jax.experimental import pallas as pl
from jax.experimental.pallas import tpu as pltpu
from jax.sharding import PartitionSpec as P

root_two_over_pi = 0.7978845608028654
cubic_coef = 0.044715
epsilon = 1e-06


def gelu_slope(preact):
    inner_term = root_two_over_pi * (preact + cubic_coef * preact * preact * preact)
    tangent = jnp.tanh(inner_term)
    gelu_value = 0.5 * preact * (1.0 + tangent)
    derivative = 0.5 * (1.0 + tangent) + 0.5 * preact * (
        1.0 - tangent * tangent
    ) * root_two_over_pi * (1.0 + 3.0 * cubic_coef * preact * preact)
    return (gelu_value, derivative)


def dequantize(weight_values, weight_scales):
    row_count, features = weight_values.shape
    blocks = weight_scales.shape[1]
    expanded = (
        weight_values.astype(jnp.float32).reshape(row_count, blocks, features // blocks)
        * weight_scales.astype(jnp.float32)[:, :, None]
    )
    return expanded.reshape(row_count, features).astype(jnp.bfloat16)


def modulate(tokens, timesteps, table):
    samples = timesteps.shape[0]
    step_count = table.shape[0]
    features = tokens.shape[1]
    onehot = (timesteps[:, None] == jnp.arange(step_count, dtype=jnp.int32)[None, :]).astype(
        jnp.float32
    )
    picked = jnp.dot(
        onehot, table.reshape(step_count, 2 * features), precision=lax.Precision.HIGHEST
    )
    picked = picked.reshape(samples, 2, features)
    grouped = tokens.astype(jnp.float32).reshape(samples, -1, features)
    centre = grouped - jnp.mean(grouped, axis=2, keepdims=True)
    inverse = lax.rsqrt(jnp.mean(centre * centre, axis=2, keepdims=True) + epsilon)
    normed = centre * inverse
    factor = 1.0 + picked[:, 1][:, None, :]
    moved = (normed * factor + picked[:, 0][:, None, :]).reshape(-1, features).astype(jnp.bfloat16)
    return (moved, normed, inverse, factor)


def normalize_back(grad_moved, normed, inverse, factor):
    samples = normed.shape[0]
    features = normed.shape[2]
    scaled_grad = grad_moved.reshape(samples, -1, features) * factor
    mean_grad = jnp.mean(scaled_grad, axis=2, keepdims=True)
    mean_prod = jnp.mean(scaled_grad * normed, axis=2, keepdims=True)
    result = inverse * (scaled_grad - mean_grad - normed * mean_prod)
    return result.reshape(-1, features).astype(jnp.bfloat16)


MESH = pl.DeviceIdType.MESH
KS = (1, 3, 2)
Z_ROWS, X_ROWS, Y_ROWS = 112, 96, 96
X_AT, Y_AT = Z_ROWS, Z_ROWS + X_ROWS
OWN_ROWS = Z_ROWS + X_ROWS + Y_ROWS


def flip(value, k):
    low, high = value % 2, value // 2
    if k & 1:
        low = 1 - low
    if k & 2:
        high = 1 - high
    return 2 * high + low


def place():
    replica, shard = lax.axis_index("replica"), lax.axis_index("shard")
    return (replica // 2, 2 * (replica % 2) + (shard // 2) % 2, shard // 4, shard % 2)


def device_at(x, y, z, core):
    return (2 * x + y // 2, (2 * z + y % 2) * 2 + core)


def quarter(x):
    return pl.multiple_of(jnp.minimum(512 * x, 1408), 128)


def half(y):
    return pl.multiple_of(896 * (y // 2), 128)


def part(v):
    return pl.multiple_of(256 * v, 128)


def add_rows(rows, store, loads):
    def body(step, _):
        at = pl.ds(pl.multiple_of(step * 16, 16), 16)
        total = loads[0](at).astype(jnp.float32)
        for load in loads[1:]:
            total = total + load(at).astype(jnp.float32)
        store(at, total)
        return 0

    lax.fori_loop(0, rows // 16, body, 0)


def reduce_kernel(
    product, out, own, other, zr1, zr2, zr3, xr1, xr2, xr3, yr1, yr2, yr3,
    zb, zc, xb, xc, yb, yc, pieces, local_sem, core_sem, s1, r1, s2, r2, s3, r3, s4, r4,
):
    x, y, z, core = place()

    def to(dx=0, dy=0, dz=0, dc=0):
        return device_at(flip(x, dx), flip(y, dy), flip(z, dz), 1 - core if dc else core)

    peers = [to(dc=1)]
    peers += [to(dx=k) for k in KS] + [to(dy=k) for k in KS] + [to(dz=k) for k in KS]
    peers += [to(dx=k, dy=2) for k in KS]
    barrier = pltpu.get_barrier_semaphore()
    for peer in peers:
        pl.semaphore_signal(barrier, inc=1, device_id=peer, device_id_type=MESH)
    pl.semaphore_wait(barrier, len(peers))

    started = []

    def send(src, dst, send_sem, recv_sem, peer):
        copy = pltpu.make_async_remote_copy(
            src_ref=src, dst_ref=dst, send_sem=send_sem, recv_sem=recv_sem,
            device_id=peer, device_id_type=MESH,
        )
        copy.start()
        started.append(copy)
        return copy

    order = [(zi, yi) for zi in (1, 3, 2, 0) for yi in (1, 0)]
    swaps = {}
    for n, (zi, yi) in enumerate(order):
        block = 2 * flip(z, zi) + flip(y, yi) % 2
        mine = pltpu.make_async_copy(
            product.at[2 * block + core], own.at[zi, yi], local_sem.at[n]
        )
        mine.start()
        theirs = send(
            product.at[2 * block + 1 - core], other.at[zi, yi],
            core_sem.at[0, n], core_sem.at[1, n], to(dc=1),
        )
        swaps[zi, yi] = (mine, theirs)

    first = {"z": [], "x": [], "y": []}
    for zi, yi in order:
        mine, theirs = swaps[zi, yi]
        mine.wait()
        theirs.wait_recv()
        mine_ref, other_ref = own.at[zi, yi], other.at[zi, yi]

        def keep(at, total, mine_ref=mine_ref):
            mine_ref[at, :] = total.astype(jnp.bfloat16)

        add_rows(
            OWN_ROWS, keep,
            [lambda at, ref=mine_ref: ref[at, :], lambda at, ref=other_ref: ref[at, :]],
        )
        if zi:
            n = (zi - 1) * 2 + yi
            first["z"].append(send(
                own.at[zi, yi, pl.ds(0, Z_ROWS), :], zr1.at[zi - 1, yi],
                s1.at[n], r1.at[n], to(dz=zi),
            ))
        for k in KS:
            n = 6 + (zi * 2 + yi) * 3 + k - 1
            first["x"].append(send(
                own.at[zi, yi, pl.ds(X_AT, X_ROWS), pl.ds(quarter(flip(x, k)), 512)],
                xr1.at[k - 1, zi, yi], s1.at[n], r1.at[n], to(dx=k),
            ))
        for k in (1, 3) if yi else (2,):
            n = 30 + zi * 3 + k - 1
            first["y"].append(send(
                own.at[zi, yi, pl.ds(Y_AT, Y_ROWS), pl.ds(half(flip(y, k)), 1024)],
                yr1.at[k - 1, zi], s1.at[n], r1.at[n], to(dy=k),
            ))

    def store_to(ref):
        def store(at, total):
            ref[at, :] = total.astype(jnp.bfloat16)

        return store

    def shifted(ref, base, columns):
        return lambda at: ref[pl.ds(base + at.start, at.size), columns]

    def plain(ref):
        return lambda at: ref[at, :]

    second = {"z": [], "x": [], "y": []}
    for copy in first["z"]:
        copy.wait_recv()
    for yi in (0, 1):
        add_rows(
            Z_ROWS, store_to(zb.at[yi]),
            [plain(own.at[0, yi])] + [plain(zr1.at[k - 1, yi]) for k in KS],
        )
    for k in KS:
        second["z"].append(send(
            zb.at[:, :, pl.ds(quarter(flip(x, k)), 512)], zr2.at[k - 1],
            s2.at[k - 1], r2.at[k - 1], to(dx=k),
        ))
    for copy in first["y"]:
        copy.wait_recv()
    for zi in (1, 3, 2, 0):
        columns = pl.ds(half(y), 1024)
        add_rows(
            Y_ROWS, store_to(yb.at[zi]),
            [shifted(own.at[zi, 0], Y_AT, columns)] + [plain(yr1.at[k - 1, zi]) for k in KS],
        )
        if zi:
            second["y"].append(send(
                yb.at[zi], yr2.at[zi - 1], s2.at[2 + zi], r2.at[2 + zi], to(dz=zi)
            ))
    for copy in first["x"]:
        copy.wait_recv()
    for yi in (1, 0):
        for zi in range(4):
            columns = pl.ds(quarter(x), 512)
            add_rows(
                X_ROWS, store_to(xb.at[zi, yi]),
                [shifted(own.at[zi, yi], X_AT, columns)]
                + [plain(xr1.at[k - 1, zi, yi]) for k in KS],
            )
        for k in (1, 3) if yi else (2,):
            second["x"].append(send(
                xb.at[:, yi, :, pl.ds(part(flip(y, k) // 2), 256)], xr2.at[k - 1],
                s2.at[5 + k], r2.at[5 + k], to(dy=k),
            ))

    third = {"z": [], "x": [], "y": []}
    for copy in second["z"]:
        copy.wait_recv()
    for yi in (1, 0):
        columns = pl.ds(quarter(x), 512)
        add_rows(
            Z_ROWS, store_to(zc.at[yi]),
            [shifted(zb.at[yi], 0, columns)] + [plain(zr2.at[k - 1, yi]) for k in KS],
        )
        for k in (1, 3) if yi else (2,):
            third["z"].append(send(
                zc.at[yi, :, pl.ds(part(flip(y, k) // 2), 256)], zr3.at[k - 1],
                s3.at[k - 1], r3.at[k - 1], to(dy=k),
            ))
    for copy in second["y"]:
        copy.wait_recv()
    add_rows(Y_ROWS, store_to(yc), [plain(yb.at[0])] + [plain(yr2.at[k - 1]) for k in KS])
    for k in KS:
        third["y"].append(send(
            yc.at[:, pl.ds(part(flip(x, k)), 256)], yr3.at[k - 1],
            s3.at[2 + k], r3.at[2 + k], to(dx=k),
        ))
    for copy in second["x"]:
        copy.wait_recv()
    for zi in (1, 3, 2, 0):
        columns = pl.ds(part(y // 2), 256)
        add_rows(
            X_ROWS, store_to(xc.at[zi]),
            [shifted(xb.at[zi, 0], 0, columns)] + [plain(xr2.at[k - 1, zi]) for k in KS],
        )
        if zi:
            third["x"].append(send(
                xc.at[zi], xr3.at[zi - 1], s3.at[5 + zi], r3.at[5 + zi], to(dz=zi)
            ))

    def store_piece(base):
        def store(at, total):
            pieces[0, pl.ds(base + at.start, at.size), :] = total.astype(jnp.bfloat16)

        return store

    for copy in third["z"]:
        copy.wait_recv()
    columns = pl.ds(part(y // 2), 256)
    add_rows(
        Z_ROWS, store_piece(0),
        [shifted(zc.at[0], 0, columns)] + [plain(zr3.at[k - 1]) for k in KS],
    )
    for copy in third["y"]:
        copy.wait_recv()
    own_columns = pl.ds(part(x), 256)
    add_rows(
        Y_ROWS, store_piece(Y_AT),
        [shifted(yc, 0, own_columns)] + [plain(yr3.at[k - 1]) for k in KS],
    )
    for copy in third["x"]:
        copy.wait_recv()
    add_rows(
        X_ROWS, store_piece(X_AT), [plain(xc.at[0])] + [plain(xr3.at[k - 1]) for k in KS]
    )

    spread = []
    for dx in (0, 1, 3, 2):
        for dy in (2, 0):
            if dx or dy:
                n = 2 * dx + dy // 2
                spread.append(send(
                    pieces.at[0], pieces.at[n], s4.at[n - 1], r4.at[n - 1], to(dx=dx, dy=dy)
                ))
    for copy in spread:
        copy.wait_recv()
    for px in range(4):
        for ph in range(2):
            lows = (px % 2 + x % 2) % 2
            highs = (px // 2 + x // 2) % 2
            slot = 2 * (2 * highs + lows) + (ph + y // 2) % 2
            at = min(512 * px, 1408) + 256 * ph
            out[0:Y_AT, at : at + 256] = pieces[slot, 0:Y_AT, :].astype(jnp.float32)
    for ph in range(2):
        for px in range(4):
            lows = (px % 2 + x % 2) % 2
            highs = (px // 2 + x // 2) % 2
            slot = 2 * (2 * highs + lows) + (ph + y // 2) % 2
            at = 896 * ph + 256 * px
            out[Y_AT:OWN_ROWS, at : at + 256] = pieces[slot, Y_AT:OWN_ROWS, :].astype(jnp.float32)
    for copy in started:
        copy.wait_send()


def reduce_blocks(product):
    features = product.shape[1]
    bf16 = jnp.bfloat16
    shapes = [
        (4, 2, OWN_ROWS, features), (4, 2, OWN_ROWS, features),
        (3, 2, Z_ROWS, features), (3, 2, Z_ROWS, 512), (3, Z_ROWS, 256),
        (3, 4, 2, X_ROWS, 512), (3, 4, X_ROWS, 256), (3, X_ROWS, 256),
        (3, 4, Y_ROWS, 1024), (3, Y_ROWS, 1024), (3, Y_ROWS, 256),
        (2, Z_ROWS, features), (2, Z_ROWS, 512),
        (4, 2, X_ROWS, 512), (4, X_ROWS, 256),
        (4, Y_ROWS, 1024), (Y_ROWS, 1024),
        (8, OWN_ROWS, 256),
    ]
    sems = [(8,), (2, 8), (42,), (42,), (9,), (9,), (9,), (9,), (7,), (7,)]
    return pl.pallas_call(
        reduce_kernel,
        out_shape=jax.ShapeDtypeStruct((OWN_ROWS, features), jnp.float32),
        in_specs=[pl.BlockSpec(memory_space=pl.ANY)],
        out_specs=pl.BlockSpec(memory_space=pltpu.VMEM),
        scratch_shapes=[pltpu.VMEM(shape, bf16) for shape in shapes]
        + [pltpu.SemaphoreType.DMA(shape) for shape in sems],
        compiler_params=pltpu.CompilerParams(
            collective_id=0, has_side_effects=True, vmem_limit_bytes=56 << 20
        ),
        name="reduce_blocks",
    )(product.reshape(-1, OWN_ROWS, features))


def per_device(tokens, timesteps, table, weight_values, weight_scales, cotangent):
    moved, normed, inverse, factor = modulate(tokens, timesteps, table)
    upstream = cotangent.astype(jnp.float32)
    weight = lax.all_gather(
        dequantize(weight_values, weight_scales), "shard", axis=0, tiled=True
    )
    preact = jnp.einsum("td,fd->tf", moved, weight, preferred_element_type=jnp.float32)
    gelu_value, derivative = gelu_slope(preact)
    hidden = gelu_value.astype(jnp.bfloat16)
    grad_pre = (upstream * derivative).astype(jnp.bfloat16)
    grad_moved = jnp.dot(grad_pre, weight, preferred_element_type=jnp.float32)
    product = lax.dot_general(
        grad_pre, moved, (((0,), (0,)), ((), ())), preferred_element_type=jnp.float32
    )
    grad_weight = reduce_blocks(product.astype(jnp.bfloat16))
    grad_tokens = normalize_back(grad_moved, normed, inverse, factor)
    return (hidden, grad_weight, grad_tokens)


def solution(mesh):
    placed = (
        P(("replica", "shard"), None),
        P(("replica", "shard")),
        P(),
        P("shard", None),
        P("shard", None),
        P(("replica", "shard"), None),
    )
    return jax.shard_map(
        per_device,
        mesh=mesh,
        in_specs=placed,
        out_specs=(P(("replica", "shard"), None), P("shard", None), P(("replica", "shard"), None)),
        check_vma=False,
    )
```

```python
import jax
import jax.numpy as jnp
from jax import lax
from jax.experimental import pallas as pl
from jax.experimental.pallas import tpu as pltpu
from jax.sharding import PartitionSpec as P

root_two_over_pi = 0.7978845608028654
cubic_coef = 0.044715
epsilon = 1e-06


def gelu_slope(preact):
    inner_term = root_two_over_pi * (preact + cubic_coef * preact * preact * preact)
    tangent = jnp.tanh(inner_term)
    gelu_value = 0.5 * preact * (1.0 + tangent)
    derivative = 0.5 * (1.0 + tangent) + 0.5 * preact * (
        1.0 - tangent * tangent
    ) * root_two_over_pi * (1.0 + 3.0 * cubic_coef * preact * preact)
    return (gelu_value, derivative)


def dequantize(weight_values, weight_scales):
    row_count, features = weight_values.shape
    blocks = weight_scales.shape[1]
    expanded = (
        weight_values.astype(jnp.float32).reshape(row_count, blocks, features // blocks)
        * weight_scales.astype(jnp.float32)[:, :, None]
    )
    return expanded.reshape(row_count, features).astype(jnp.bfloat16)


def modulate(tokens, timesteps, table):
    samples = timesteps.shape[0]
    step_count = table.shape[0]
    features = tokens.shape[1]
    onehot = (timesteps[:, None] == jnp.arange(step_count, dtype=jnp.int32)[None, :]).astype(
        jnp.float32
    )
    picked = jnp.dot(
        onehot, table.reshape(step_count, 2 * features), precision=lax.Precision.HIGHEST
    )
    picked = picked.reshape(samples, 2, features)
    grouped = tokens.astype(jnp.float32).reshape(samples, -1, features)
    centre = grouped - jnp.mean(grouped, axis=2, keepdims=True)
    inverse = lax.rsqrt(jnp.mean(centre * centre, axis=2, keepdims=True) + epsilon)
    normed = centre * inverse
    factor = 1.0 + picked[:, 1][:, None, :]
    moved = (normed * factor + picked[:, 0][:, None, :]).reshape(-1, features).astype(jnp.bfloat16)
    return (moved, normed, inverse, factor)


def normalize_back(grad_moved, normed, inverse, factor):
    samples = normed.shape[0]
    features = normed.shape[2]
    scaled_grad = grad_moved.reshape(samples, -1, features) * factor
    mean_grad = jnp.mean(scaled_grad, axis=2, keepdims=True)
    mean_prod = jnp.mean(scaled_grad * normed, axis=2, keepdims=True)
    result = inverse * (scaled_grad - mean_grad - normed * mean_prod)
    return result.reshape(-1, features).astype(jnp.bfloat16)


MESH = pl.DeviceIdType.MESH
KS = (1, 3, 2)
Z_ROWS, X_ROWS, Y_ROWS = 112, 96, 96
X_AT, Y_AT = Z_ROWS, Z_ROWS + X_ROWS
OWN_ROWS = Z_ROWS + X_ROWS + Y_ROWS
WINDOWS = ((0, 1024), (1024, 1024), (2048, 1024), (3072, 1024), (4096, 768))


def flip(value, k):
    low, high = value % 2, value // 2
    if k & 1:
        low = 1 - low
    if k & 2:
        high = 1 - high
    return 2 * high + low


def place():
    replica, shard = lax.axis_index("replica"), lax.axis_index("shard")
    return (replica // 2, 2 * (replica % 2) + (shard // 2) % 2, shard // 4, shard % 2)


def device_at(x, y, z, core):
    return (2 * x + y // 2, (2 * z + y % 2) * 2 + core)


def quarter(x):
    return pl.multiple_of(jnp.minimum(512 * x, 1408), 128)


def half(y):
    return pl.multiple_of(896 * (y // 2), 128)


def part(v):
    return pl.multiple_of(256 * v, 128)


def add_rows(rows, store, loads):
    def body(step, _):
        at = pl.ds(pl.multiple_of(step * 16, 16), 16)
        total = loads[0](at).astype(jnp.float32)
        for load in loads[1:]:
            total = total + load(at).astype(jnp.float32)
        store(at, total)
        return 0

    lax.fori_loop(0, rows // 16, body, 0)


def reduce_kernel(
    gradient_rows, gradient, moved, weight, out, grad_moved, own, operand, tokens_all,
    weight_parts, gradient_parts, zr1, zr2, zr3, xr1, xr2, xr3, yr1, yr2, yr3,
    zb, zc, xb, xc, yb, yc, pieces, local_sem, core_sem, part_sem, s1, r1, s2, r2, s3, r3, s4, r4,
):
    x, y, z, core = place()

    def to(dx=0, dy=0, dz=0, dc=0):
        return device_at(flip(x, dx), flip(y, dy), flip(z, dz), 1 - core if dc else core)

    peers = [to(dc=1)]
    peers += [to(dx=k) for k in KS] + [to(dy=k) for k in KS] + [to(dz=k) for k in KS]
    peers += [to(dx=k, dy=2) for k in KS]
    barrier = pltpu.get_barrier_semaphore()
    for peer in peers:
        pl.semaphore_signal(barrier, inc=1, device_id=peer, device_id_type=MESH)
    pl.semaphore_wait(barrier, len(peers))

    started = []

    def send(src, dst, send_sem, recv_sem, peer):
        copy = pltpu.make_async_remote_copy(
            src_ref=src, dst_ref=dst, send_sem=send_sem, recv_sem=recv_sem,
            device_id=peer, device_id_type=MESH,
        )
        copy.start()
        started.append(copy)
        return copy

    def fetch(w):
        at, size = WINDOWS[w]
        return [
            pltpu.make_async_copy(
                weight.at[pl.ds(at, size), :],
                weight_parts.at[w % 2, pl.ds(0, size), :],
                part_sem.at[0, w % 2],
            ),
            pltpu.make_async_copy(
                gradient.at[:, pl.ds(at, size)],
                gradient_parts.at[w % 2, :, pl.ds(0, size)],
                part_sem.at[1, w % 2],
            ),
        ]

    tokens = moved.shape[0]
    lanes = pl.ds(pl.multiple_of(core * tokens, 128), tokens)
    mine_moved = pltpu.make_async_copy(moved, tokens_all.at[lanes, :], local_sem.at[8])
    mine_moved.start()
    their_moved = send(
        moved, tokens_all.at[lanes, :], core_sem.at[0, 8], core_sem.at[1, 8], to(dc=1)
    )
    swaps = {}
    order = [(zi, yi) for zi in (1, 3, 2, 0) for yi in (1, 0)]
    for n, (zi, yi) in enumerate(order):
        block = 2 * flip(z, zi) + flip(y, yi) % 2
        mine = pltpu.make_async_copy(
            gradient_rows.at[2 * block + core], operand.at[zi, yi, :, lanes], local_sem.at[n]
        )
        mine.start()
        theirs = send(
            gradient_rows.at[2 * block + 1 - core], operand.at[zi, yi, :, lanes],
            core_sem.at[0, n], core_sem.at[1, n], to(dc=1),
        )
        swaps[zi, yi] = (mine, theirs)
    windows = [fetch(0), fetch(1)]
    for pair in windows:
        for copy in pair:
            copy.start()
    mine_moved.wait()
    their_moved.wait_recv()

    first = {"z": [], "x": [], "y": []}
    for zi, yi in order:
        if yi:
            for each in (1, 0):
                mine, theirs = swaps[zi, each]
                mine.wait()
                theirs.wait_recv()
            rows = operand[zi].reshape(2 * OWN_ROWS, 2 * tokens)
            for at, size in ((0, 1024), (1024, 896)):
                term = jnp.dot(
                    rows, tokens_all[:, at : at + size], preferred_element_type=jnp.float32
                )
                own[zi, :, :, at : at + size] = term.astype(jnp.bfloat16).reshape(
                    2, OWN_ROWS, size
                )
        if zi:
            n = (zi - 1) * 2 + yi
            first["z"].append(send(
                own.at[zi, yi, pl.ds(0, Z_ROWS), :], zr1.at[zi - 1, yi],
                s1.at[n], r1.at[n], to(dz=zi),
            ))
        for k in KS:
            n = 6 + (zi * 2 + yi) * 3 + k - 1
            first["x"].append(send(
                own.at[zi, yi, pl.ds(X_AT, X_ROWS), pl.ds(quarter(flip(x, k)), 512)],
                xr1.at[k - 1, zi, yi], s1.at[n], r1.at[n], to(dx=k),
            ))
        for k in (1, 3) if yi else (2,):
            n = 30 + zi * 3 + k - 1
            first["y"].append(send(
                own.at[zi, yi, pl.ds(Y_AT, Y_ROWS), pl.ds(half(flip(y, k)), 1024)],
                yr1.at[k - 1, zi], s1.at[n], r1.at[n], to(dy=k),
            ))

    for w in range(len(WINDOWS)):
        for copy in windows[w]:
            copy.wait()
        size = WINDOWS[w][1]
        for at, width in ((0, 1024), (1024, 896)):
            term = jnp.dot(
                gradient_parts[w % 2, :, 0:size],
                weight_parts[w % 2, 0:size, at : at + width],
                preferred_element_type=jnp.float32,
            )
            columns = slice(at, at + width)
            grad_moved[:, columns] = term if w == 0 else grad_moved[:, columns] + term
        if w + 2 < len(WINDOWS):
            windows.append(fetch(w + 2))
            for copy in windows[w + 2]:
                copy.start()

    def store_to(ref):
        def store(at, total):
            ref[at, :] = total.astype(jnp.bfloat16)

        return store

    def shifted(ref, base, columns):
        return lambda at: ref[pl.ds(base + at.start, at.size), columns]

    def plain(ref):
        return lambda at: ref[at, :]

    second = {"z": [], "x": [], "y": []}
    for copy in first["z"]:
        copy.wait_recv()
    for yi in (0, 1):
        add_rows(
            Z_ROWS, store_to(zb.at[yi]),
            [plain(own.at[0, yi])] + [plain(zr1.at[k - 1, yi]) for k in KS],
        )
    for k in KS:
        second["z"].append(send(
            zb.at[:, :, pl.ds(quarter(flip(x, k)), 512)], zr2.at[k - 1],
            s2.at[k - 1], r2.at[k - 1], to(dx=k),
        ))
    for copy in first["y"]:
        copy.wait_recv()
    for zi in (1, 3, 2, 0):
        columns = pl.ds(half(y), 1024)
        add_rows(
            Y_ROWS, store_to(yb.at[zi]),
            [shifted(own.at[zi, 0], Y_AT, columns)] + [plain(yr1.at[k - 1, zi]) for k in KS],
        )
        if zi:
            second["y"].append(send(
                yb.at[zi], yr2.at[zi - 1], s2.at[2 + zi], r2.at[2 + zi], to(dz=zi)
            ))
    for copy in first["x"]:
        copy.wait_recv()
    for yi in (1, 0):
        for zi in range(4):
            columns = pl.ds(quarter(x), 512)
            add_rows(
                X_ROWS, store_to(xb.at[zi, yi]),
                [shifted(own.at[zi, yi], X_AT, columns)]
                + [plain(xr1.at[k - 1, zi, yi]) for k in KS],
            )
        for k in (1, 3) if yi else (2,):
            second["x"].append(send(
                xb.at[:, yi, :, pl.ds(part(flip(y, k) // 2), 256)], xr2.at[k - 1],
                s2.at[5 + k], r2.at[5 + k], to(dy=k),
            ))

    third = {"z": [], "x": [], "y": []}
    for copy in second["z"]:
        copy.wait_recv()
    for yi in (1, 0):
        columns = pl.ds(quarter(x), 512)
        add_rows(
            Z_ROWS, store_to(zc.at[yi]),
            [shifted(zb.at[yi], 0, columns)] + [plain(zr2.at[k - 1, yi]) for k in KS],
        )
        for k in (1, 3) if yi else (2,):
            third["z"].append(send(
                zc.at[yi, :, pl.ds(part(flip(y, k) // 2), 256)], zr3.at[k - 1],
                s3.at[k - 1], r3.at[k - 1], to(dy=k),
            ))
    for copy in second["y"]:
        copy.wait_recv()
    add_rows(Y_ROWS, store_to(yc), [plain(yb.at[0])] + [plain(yr2.at[k - 1]) for k in KS])
    for k in KS:
        third["y"].append(send(
            yc.at[:, pl.ds(part(flip(x, k)), 256)], yr3.at[k - 1],
            s3.at[2 + k], r3.at[2 + k], to(dx=k),
        ))
    for copy in second["x"]:
        copy.wait_recv()
    for zi in (1, 3, 2, 0):
        columns = pl.ds(part(y // 2), 256)
        add_rows(
            X_ROWS, store_to(xc.at[zi]),
            [shifted(xb.at[zi, 0], 0, columns)] + [plain(xr2.at[k - 1, zi]) for k in KS],
        )
        if zi:
            third["x"].append(send(
                xc.at[zi], xr3.at[zi - 1], s3.at[5 + zi], r3.at[5 + zi], to(dz=zi)
            ))

    def store_piece(base):
        def store(at, total):
            pieces[0, pl.ds(base + at.start, at.size), :] = total.astype(jnp.bfloat16)

        return store

    for copy in third["z"]:
        copy.wait_recv()
    columns = pl.ds(part(y // 2), 256)
    add_rows(
        Z_ROWS, store_piece(0),
        [shifted(zc.at[0], 0, columns)] + [plain(zr3.at[k - 1]) for k in KS],
    )
    for copy in third["y"]:
        copy.wait_recv()
    own_columns = pl.ds(part(x), 256)
    add_rows(
        Y_ROWS, store_piece(Y_AT),
        [shifted(yc, 0, own_columns)] + [plain(yr3.at[k - 1]) for k in KS],
    )
    for copy in third["x"]:
        copy.wait_recv()
    add_rows(
        X_ROWS, store_piece(X_AT), [plain(xc.at[0])] + [plain(xr3.at[k - 1]) for k in KS]
    )

    spread = []
    for dx in (0, 1, 3, 2):
        for dy in (2, 0):
            if dx or dy:
                n = 2 * dx + dy // 2
                spread.append(send(
                    pieces.at[0], pieces.at[n], s4.at[n - 1], r4.at[n - 1], to(dx=dx, dy=dy)
                ))
    for copy in spread:
        copy.wait_recv()
    for px in range(4):
        for ph in range(2):
            lows = (px % 2 + x % 2) % 2
            highs = (px // 2 + x // 2) % 2
            slot = 2 * (2 * highs + lows) + (ph + y // 2) % 2
            at = min(512 * px, 1408) + 256 * ph
            out[0:Y_AT, at : at + 256] = pieces[slot, 0:Y_AT, :].astype(jnp.float32)
    for ph in range(2):
        for px in range(4):
            lows = (px % 2 + x % 2) % 2
            highs = (px // 2 + x // 2) % 2
            slot = 2 * (2 * highs + lows) + (ph + y // 2) % 2
            at = 896 * ph + 256 * px
            out[Y_AT:OWN_ROWS, at : at + 256] = pieces[slot, Y_AT:OWN_ROWS, :].astype(jnp.float32)
    for copy in started:
        copy.wait_send()


def reduce_blocks(grad_pre, moved, weight):
    tokens, features = moved.shape
    bf16 = jnp.bfloat16
    shapes = [
        (4, 2, OWN_ROWS, features), (4, 2, OWN_ROWS, 2 * tokens), (2 * tokens, features),
        (2, 1024, features), (2, tokens, 1024),
        (3, 2, Z_ROWS, features), (3, 2, Z_ROWS, 512), (3, Z_ROWS, 256),
        (3, 4, 2, X_ROWS, 512), (3, 4, X_ROWS, 256), (3, X_ROWS, 256),
        (3, 4, Y_ROWS, 1024), (3, Y_ROWS, 1024), (3, Y_ROWS, 256),
        (2, Z_ROWS, features), (2, Z_ROWS, 512),
        (4, 2, X_ROWS, 512), (4, X_ROWS, 256),
        (4, Y_ROWS, 1024), (Y_ROWS, 1024),
        (8, OWN_ROWS, 256),
    ]
    sems = [(9,), (2, 9), (2, 2), (42,), (42,), (9,), (9,), (9,), (9,), (7,), (7,)]
    return pl.pallas_call(
        reduce_kernel,
        out_shape=(
            jax.ShapeDtypeStruct((OWN_ROWS, features), jnp.float32),
            jax.ShapeDtypeStruct((tokens, features), jnp.float32),
        ),
        in_specs=[pl.BlockSpec(memory_space=pl.ANY)] * 4,
        out_specs=[pl.BlockSpec(memory_space=pltpu.VMEM)] * 2,
        scratch_shapes=[pltpu.VMEM(shape, bf16) for shape in shapes]
        + [pltpu.SemaphoreType.DMA(shape) for shape in sems],
        compiler_params=pltpu.CompilerParams(
            collective_id=0, has_side_effects=True, vmem_limit_bytes=60 << 20
        ),
        name="reduce_blocks",
    )(grad_pre.T.reshape(-1, OWN_ROWS, tokens), grad_pre, moved, weight)


def per_device(tokens, timesteps, table, weight_values, weight_scales, cotangent):
    moved, normed, inverse, factor = modulate(tokens, timesteps, table)
    upstream = cotangent.astype(jnp.float32)
    weight = lax.all_gather(
        dequantize(weight_values, weight_scales), "shard", axis=0, tiled=True
    )
    preact = jnp.einsum("td,fd->tf", moved, weight, preferred_element_type=jnp.float32)
    gelu_value, derivative = gelu_slope(preact)
    hidden = gelu_value.astype(jnp.bfloat16)
    grad_pre = (upstream * derivative).astype(jnp.bfloat16)
    grad_weight, grad_moved = reduce_blocks(grad_pre, moved, weight)
    grad_tokens = normalize_back(grad_moved, normed, inverse, factor)
    return (hidden, grad_weight, grad_tokens)


def solution(mesh):
    placed = (
        P(("replica", "shard"), None),
        P(("replica", "shard")),
        P(),
        P("shard", None),
        P("shard", None),
        P(("replica", "shard"), None),
    )
    return jax.shard_map(
        per_device,
        mesh=mesh,
        in_specs=placed,
        out_specs=(P(("replica", "shard"), None), P("shard", None), P(("replica", "shard"), None)),
        check_vma=False,
    )
```

```python
import jax
import jax.numpy as jnp
from jax import lax
from jax.experimental import pallas as pl
from jax.experimental.pallas import tpu as pltpu
from jax.sharding import PartitionSpec as P

root_two_over_pi = 0.7978845608028654
cubic_coef = 0.044715
epsilon = 1e-06


def gelu_slope(preact):
    inner_term = root_two_over_pi * (preact + cubic_coef * preact * preact * preact)
    tangent = jnp.tanh(inner_term)
    gelu_value = 0.5 * preact * (1.0 + tangent)
    derivative = 0.5 * (1.0 + tangent) + 0.5 * preact * (
        1.0 - tangent * tangent
    ) * root_two_over_pi * (1.0 + 3.0 * cubic_coef * preact * preact)
    return (gelu_value, derivative)


def dequantize(weight_values, weight_scales):
    row_count, features = weight_values.shape
    blocks = weight_scales.shape[1]
    expanded = (
        weight_values.astype(jnp.float32).reshape(row_count, blocks, features // blocks)
        * weight_scales.astype(jnp.float32)[:, :, None]
    )
    return expanded.reshape(row_count, features).astype(jnp.bfloat16)


def modulate(tokens, timesteps, table):
    samples = timesteps.shape[0]
    step_count = table.shape[0]
    features = tokens.shape[1]
    onehot = (timesteps[:, None] == jnp.arange(step_count, dtype=jnp.int32)[None, :]).astype(
        jnp.float32
    )
    picked = jnp.dot(
        onehot, table.reshape(step_count, 2 * features), precision=lax.Precision.HIGHEST
    )
    picked = picked.reshape(samples, 2, features)
    grouped = tokens.astype(jnp.float32).reshape(samples, -1, features)
    centre = grouped - jnp.mean(grouped, axis=2, keepdims=True)
    inverse = lax.rsqrt(jnp.mean(centre * centre, axis=2, keepdims=True) + epsilon)
    normed = centre * inverse
    factor = 1.0 + picked[:, 1][:, None, :]
    moved = (normed * factor + picked[:, 0][:, None, :]).reshape(-1, features).astype(jnp.bfloat16)
    return (moved, factor)


MESH = pl.DeviceIdType.MESH
KS = (1, 3, 2)
Z_ROWS, X_ROWS, Y_ROWS = 112, 96, 96
X_AT, Y_AT = Z_ROWS, Z_ROWS + X_ROWS
OWN_ROWS = Z_ROWS + X_ROWS + Y_ROWS
WINDOWS = ((0, 1024), (1024, 1024), (2048, 1024), (3072, 1024), (4096, 768))


def flip(value, k):
    low, high = value % 2, value // 2
    if k & 1:
        low = 1 - low
    if k & 2:
        high = 1 - high
    return 2 * high + low


def place():
    replica, shard = lax.axis_index("replica"), lax.axis_index("shard")
    return (replica // 2, 2 * (replica % 2) + (shard // 2) % 2, shard // 4, shard % 2)


def device_at(x, y, z, core):
    return (2 * x + y // 2, (2 * z + y % 2) * 2 + core)


def quarter(x):
    return pl.multiple_of(jnp.minimum(512 * x, 1408), 128)


def half(y):
    return pl.multiple_of(896 * (y // 2), 128)


def part(v):
    return pl.multiple_of(256 * v, 128)


def add_rows(rows, store, loads):
    def body(step, _):
        at = pl.ds(pl.multiple_of(step * 16, 16), 16)
        total = loads[0](at).astype(jnp.float32)
        for load in loads[1:]:
            total = total + load(at).astype(jnp.float32)
        store(at, total)
        return 0

    lax.fori_loop(0, rows // 16, body, 0)


def reduce_kernel(
    gradient_rows, gradient, moved, weight, tokens, factor, out, grad_tokens, grad_moved, own, operand, tokens_all,
    weight_parts, gradient_parts, zr1, zr2, zr3, xr1, xr2, xr3, yr1, yr2, yr3,
    zb, zc, xb, xc, yb, yc, pieces, local_sem, core_sem, part_sem, s1, r1, s2, r2, s3, r3, s4, r4,
):
    x, y, z, core = place()

    def to(dx=0, dy=0, dz=0, dc=0):
        return device_at(flip(x, dx), flip(y, dy), flip(z, dz), 1 - core if dc else core)

    peers = [to(dc=1)]
    peers += [to(dx=k) for k in KS] + [to(dy=k) for k in KS] + [to(dz=k) for k in KS]
    barrier = pltpu.get_barrier_semaphore()
    for peer in peers:
        pl.semaphore_signal(barrier, inc=1, device_id=peer, device_id_type=MESH)
    pl.semaphore_wait(barrier, len(peers))

    started = []

    def send(src, dst, send_sem, recv_sem, peer):
        copy = pltpu.make_async_remote_copy(
            src_ref=src, dst_ref=dst, send_sem=send_sem, recv_sem=recv_sem,
            device_id=peer, device_id_type=MESH,
        )
        copy.start()
        started.append(copy)
        return copy

    def fetch(w):
        at, size = WINDOWS[w]
        return [
            pltpu.make_async_copy(
                weight.at[pl.ds(at, size), :],
                weight_parts.at[w % 2, pl.ds(0, size), :],
                part_sem.at[0, w % 2],
            ),
            pltpu.make_async_copy(
                gradient.at[:, pl.ds(at, size)],
                gradient_parts.at[w % 2, :, pl.ds(0, size)],
                part_sem.at[1, w % 2],
            ),
        ]

    count = moved.shape[0]
    lanes = pl.ds(pl.multiple_of(core * count, 128), count)
    mine_moved = pltpu.make_async_copy(moved, tokens_all.at[lanes, :], local_sem.at[8])
    mine_moved.start()
    their_moved = send(
        moved, tokens_all.at[lanes, :], core_sem.at[0, 8], core_sem.at[1, 8], to(dc=1)
    )
    swaps = {}
    order = [(zi, yi) for zi in (1, 3, 2, 0) for yi in (1, 0)]
    for n, (zi, yi) in enumerate(order):
        block = 2 * flip(z, zi) + flip(y, yi) % 2
        mine = pltpu.make_async_copy(
            gradient_rows.at[2 * block + core], operand.at[zi, yi, :, lanes], local_sem.at[n]
        )
        mine.start()
        theirs = send(
            gradient_rows.at[2 * block + 1 - core], operand.at[zi, yi, :, lanes],
            core_sem.at[0, n], core_sem.at[1, n], to(dc=1),
        )
        swaps[zi, yi] = (mine, theirs)
    windows = [fetch(0), fetch(1)]
    for pair in windows:
        for copy in pair:
            copy.start()
    mine_moved.wait()
    their_moved.wait_recv()

    first = {"z": [], "x": [], "y": []}
    for zi, yi in order:
        if yi:
            for each in (1, 0):
                mine, theirs = swaps[zi, each]
                mine.wait()
                theirs.wait_recv()
            rows = operand[zi].reshape(2 * OWN_ROWS, 2 * count)
            for at, size in ((0, 1024), (1024, 896)):
                term = jnp.dot(
                    rows, tokens_all[:, at : at + size], preferred_element_type=jnp.float32
                )
                own[zi, :, :, at : at + size] = term.astype(jnp.bfloat16).reshape(
                    2, OWN_ROWS, size
                )
        if zi:
            n = (zi - 1) * 2 + yi
            first["z"].append(send(
                own.at[zi, yi, pl.ds(0, Z_ROWS), :], zr1.at[zi - 1, yi],
                s1.at[n], r1.at[n], to(dz=zi),
            ))
        for k in KS:
            n = 6 + (zi * 2 + yi) * 3 + k - 1
            first["x"].append(send(
                own.at[zi, yi, pl.ds(X_AT, X_ROWS), pl.ds(quarter(flip(x, k)), 512)],
                xr1.at[k - 1, zi, yi], s1.at[n], r1.at[n], to(dx=k),
            ))
        for k in (1, 3) if yi else (2,):
            n = 30 + zi * 3 + k - 1
            first["y"].append(send(
                own.at[zi, yi, pl.ds(Y_AT, Y_ROWS), pl.ds(half(flip(y, k)), 1024)],
                yr1.at[k - 1, zi], s1.at[n], r1.at[n], to(dy=k),
            ))

    for w in range(len(WINDOWS)):
        for copy in windows[w]:
            copy.wait()
        size = WINDOWS[w][1]
        for at, width in ((0, 1024), (1024, 896)):
            term = jnp.dot(
                gradient_parts[w % 2, :, 0:size],
                weight_parts[w % 2, 0:size, at : at + width],
                preferred_element_type=jnp.float32,
            )
            columns = slice(at, at + width)
            grad_moved[:, columns] = term if w == 0 else grad_moved[:, columns] + term
        if w + 2 < len(WINDOWS):
            windows.append(fetch(w + 2))
            for copy in windows[w + 2]:
                copy.start()

    def store_to(ref):
        def store(at, total):
            ref[at, :] = total.astype(jnp.bfloat16)

        return store

    def shifted(ref, base, columns):
        return lambda at: ref[pl.ds(base + at.start, at.size), columns]

    def plain(ref):
        return lambda at: ref[at, :]

    second = {"z": [], "x": [], "y": []}
    for copy in first["z"]:
        copy.wait_recv()
    for yi in (0, 1):
        add_rows(
            Z_ROWS, store_to(zb.at[yi]),
            [plain(own.at[0, yi])] + [plain(zr1.at[k - 1, yi]) for k in KS],
        )
    for k in KS:
        second["z"].append(send(
            zb.at[:, :, pl.ds(quarter(flip(x, k)), 512)], zr2.at[k - 1],
            s2.at[k - 1], r2.at[k - 1], to(dx=k),
        ))
    for copy in first["y"]:
        copy.wait_recv()
    for zi in (1, 3, 2, 0):
        columns = pl.ds(half(y), 1024)
        add_rows(
            Y_ROWS, store_to(yb.at[zi]),
            [shifted(own.at[zi, 0], Y_AT, columns)] + [plain(yr1.at[k - 1, zi]) for k in KS],
        )
        if zi:
            second["y"].append(send(
                yb.at[zi], yr2.at[zi - 1], s2.at[2 + zi], r2.at[2 + zi], to(dz=zi)
            ))
    for copy in first["x"]:
        copy.wait_recv()
    for yi in (1, 0):
        for zi in range(4):
            columns = pl.ds(quarter(x), 512)
            add_rows(
                X_ROWS, store_to(xb.at[zi, yi]),
                [shifted(own.at[zi, yi], X_AT, columns)]
                + [plain(xr1.at[k - 1, zi, yi]) for k in KS],
            )
        for k in (1, 3) if yi else (2,):
            second["x"].append(send(
                xb.at[:, yi, :, pl.ds(part(flip(y, k) // 2), 256)], xr2.at[k - 1],
                s2.at[5 + k], r2.at[5 + k], to(dy=k),
            ))

    per_sample = count // factor.shape[0]

    def finish(step, _):
        at = pl.ds(pl.multiple_of(step * 16, 16), 16)
        value = tokens[at, :].astype(jnp.float32)
        centre = value - jnp.mean(value, axis=1, keepdims=True)
        inverse = lax.rsqrt(jnp.mean(centre * centre, axis=1, keepdims=True) + epsilon)
        normed = centre * inverse
        scaled_grad = grad_moved[at, :] * factor[pl.ds(step * 16 // per_sample, 1), :]
        mean_grad = jnp.mean(scaled_grad, axis=1, keepdims=True)
        mean_prod = jnp.mean(scaled_grad * normed, axis=1, keepdims=True)
        result = inverse * (scaled_grad - mean_grad - normed * mean_prod)
        grad_tokens[at, :] = result.astype(jnp.bfloat16)
        return 0

    lax.fori_loop(0, count // 16, finish, 0)

    third = {"z": [], "x": [], "y": []}
    for copy in second["z"]:
        copy.wait_recv()
    for yi in (1, 0):
        columns = pl.ds(quarter(x), 512)
        add_rows(
            Z_ROWS, store_to(zc.at[yi]),
            [shifted(zb.at[yi], 0, columns)] + [plain(zr2.at[k - 1, yi]) for k in KS],
        )
        for k in (1, 3) if yi else (2,):
            third["z"].append(send(
                zc.at[yi, :, pl.ds(part(flip(y, k) // 2), 256)], zr3.at[k - 1],
                s3.at[k - 1], r3.at[k - 1], to(dy=k),
            ))
    for copy in second["y"]:
        copy.wait_recv()
    add_rows(Y_ROWS, store_to(yc), [plain(yb.at[0])] + [plain(yr2.at[k - 1]) for k in KS])
    for k in KS:
        third["y"].append(send(
            yc.at[:, pl.ds(part(flip(x, k)), 256)], yr3.at[k - 1],
            s3.at[2 + k], r3.at[2 + k], to(dx=k),
        ))
    for copy in second["x"]:
        copy.wait_recv()
    for zi in (1, 3, 2, 0):
        columns = pl.ds(part(y // 2), 256)
        add_rows(
            X_ROWS, store_to(xc.at[zi]),
            [shifted(xb.at[zi, 0], 0, columns)] + [plain(xr2.at[k - 1, zi]) for k in KS],
        )
        if zi:
            third["x"].append(send(
                xc.at[zi], xr3.at[zi - 1], s3.at[5 + zi], r3.at[5 + zi], to(dz=zi)
            ))

    def store_piece(base):
        def store(at, total):
            pieces[0, pl.ds(base + at.start, at.size), :] = total.astype(jnp.bfloat16)

        return store

    for copy in third["z"]:
        copy.wait_recv()
    columns = pl.ds(part(y // 2), 256)
    add_rows(
        Z_ROWS, store_piece(0),
        [shifted(zc.at[0], 0, columns)] + [plain(zr3.at[k - 1]) for k in KS],
    )
    for copy in third["y"]:
        copy.wait_recv()
    own_columns = pl.ds(part(x), 256)
    add_rows(
        Y_ROWS, store_piece(Y_AT),
        [shifted(yc, 0, own_columns)] + [plain(yr3.at[k - 1]) for k in KS],
    )
    for copy in third["x"]:
        copy.wait_recv()
    add_rows(
        X_ROWS, store_piece(X_AT), [plain(xc.at[0])] + [plain(xr3.at[k - 1]) for k in KS]
    )

    def hand(source, slot, peer):
        return send(
            pieces.at[source], pieces.at[slot], s4.at[slot - 1], r4.at[slot - 1], peer
        )

    along = {k: hand(0, 2 * k, to(dx=k)) for k in KS}
    across = [hand(0, 1, to(dy=2))]
    for k in KS:
        along[k].wait_recv()
        across.append(hand(2 * k, 2 * k + 1, to(dy=2)))
    for copy in across:
        copy.wait_recv()
    for px in range(4):
        for ph in range(2):
            lows = (px % 2 + x % 2) % 2
            highs = (px // 2 + x // 2) % 2
            slot = 2 * (2 * highs + lows) + (ph + y // 2) % 2
            at = min(512 * px, 1408) + 256 * ph
            out[0:Y_AT, at : at + 256] = pieces[slot, 0:Y_AT, :].astype(jnp.float32)
    for ph in range(2):
        for px in range(4):
            lows = (px % 2 + x % 2) % 2
            highs = (px // 2 + x // 2) % 2
            slot = 2 * (2 * highs + lows) + (ph + y // 2) % 2
            at = 896 * ph + 256 * px
            out[Y_AT:OWN_ROWS, at : at + 256] = pieces[slot, Y_AT:OWN_ROWS, :].astype(jnp.float32)
    for copy in started:
        copy.wait_send()


def reduce_blocks(grad_pre, moved, weight, tokens, factor):
    count, features = moved.shape
    bf16 = jnp.bfloat16
    shapes = [
        (4, 2, OWN_ROWS, features), (4, 2, OWN_ROWS, 2 * count), (2 * count, features),
        (2, 1024, features), (2, count, 1024),
        (3, 2, Z_ROWS, features), (3, 2, Z_ROWS, 512), (3, Z_ROWS, 256),
        (3, 4, 2, X_ROWS, 512), (3, 4, X_ROWS, 256), (3, X_ROWS, 256),
        (3, 4, Y_ROWS, 1024), (3, Y_ROWS, 1024), (3, Y_ROWS, 256),
        (2, Z_ROWS, features), (2, Z_ROWS, 512),
        (4, 2, X_ROWS, 512), (4, X_ROWS, 256),
        (4, Y_ROWS, 1024), (Y_ROWS, 1024),
        (8, OWN_ROWS, 256),
    ]
    sems = [(9,), (2, 9), (2, 2), (42,), (42,), (9,), (9,), (9,), (9,), (7,), (7,)]
    return pl.pallas_call(
        reduce_kernel,
        out_shape=(
            jax.ShapeDtypeStruct((OWN_ROWS, features), jnp.float32),
            jax.ShapeDtypeStruct((count, features), bf16),
        ),
        in_specs=[pl.BlockSpec(memory_space=pl.ANY)] * 4
        + [pl.BlockSpec(memory_space=pltpu.VMEM)] * 2,
        out_specs=[pl.BlockSpec(memory_space=pltpu.VMEM)] * 2,
        scratch_shapes=[pltpu.VMEM((count, features), jnp.float32)]
        + [pltpu.VMEM(shape, bf16) for shape in shapes]
        + [pltpu.SemaphoreType.DMA(shape) for shape in sems],
        compiler_params=pltpu.CompilerParams(
            collective_id=0, has_side_effects=True, vmem_limit_bytes=60 << 20
        ),
        name="reduce_blocks",
    )(grad_pre.T.reshape(-1, OWN_ROWS, count), grad_pre, moved, weight, tokens, factor)


GX_ROWS, GZ_ROWS, GY_ROWS = 128, 32, 144
GX_PART = GX_ROWS // 4
GY_AT = GX_ROWS + GZ_ROWS
HALVES = {1: (0, 1024), 3: (1024, 896)}


def gather_kernel(mine, whole, own_sem, ss, rs):
    x, y, z, core = place()

    def to(dx=0, dy=0, dz=0, dc=0):
        return device_at(flip(x, dx), flip(y, dy), flip(z, dz), 1 - core if dc else core)

    peers = [to(dc=1)]
    peers += [to(dx=k) for k in KS] + [to(dy=k) for k in (1, 3)] + [to(dz=k) for k in KS]
    barrier = pltpu.get_barrier_semaphore()
    for peer in peers:
        pl.semaphore_signal(barrier, inc=1, device_id=peer, device_id_type=MESH)
    pl.semaphore_wait(barrier, len(peers))

    started, shared = [], []

    def send(source, block, rows, columns, peer):
        n = len(started)
        copy = pltpu.make_async_remote_copy(
            src_ref=source.at[rows, columns],
            dst_ref=whole.at[block, rows, columns],
            send_sem=ss.at[n], recv_sem=rs.at[n],
            device_id=peer, device_id_type=MESH,
        )
        copy.start()
        started.append(copy)
        return copy

    every = slice(None)

    def block_of(zi, yi):
        return 2 * (2 * flip(z, zi) + flip(y, yi) % 2) + core

    own = block_of(0, 0)
    keep = pltpu.make_async_copy(mine, whole.at[own], own_sem)
    keep.start()

    def share(source, block, rows, columns):
        shared.append(send(source, block, rows, columns, to(dc=1)))

    xpart = pl.ds(pl.multiple_of(GX_PART * x, 8), GX_PART)
    zrows, yrows, zyrows = pl.ds(GX_ROWS, GZ_ROWS), pl.ds(GY_AT, GY_ROWS), pl.ds(GX_ROWS, GZ_ROWS + GY_ROWS)
    cols = {k: pl.ds(*HALVES[k]) for k in HALVES}

    xz, xy, xx, zyz, yy, zy, zz = {}, {}, {}, {}, {}, {}, {}

    def x_down(zi, yi, source):
        for k in KS:
            xx[zi, yi, k] = send(source, block_of(zi, yi), xpart, every, to(dx=k))

    def x_across(zi, source):
        for k in (1, 3):
            xy[zi, k] = send(source, block_of(zi, 0), xpart, cols[k], to(dy=k))

    def y_across(zi, source):
        for k in (1, 3):
            yy[zi, k] = send(source, block_of(zi, 0), yrows, cols[k], to(dy=k))

    for k in KS:
        xz[k] = send(mine, own, xpart, every, to(dz=k))
    x_across(0, mine)
    zyz[1] = send(mine, own, zyrows, every, to(dz=1))
    for k in (1, 3):
        zy[k] = send(mine, own, zrows, cols[k], to(dy=k))
    y_across(0, mine)
    zyz[3] = send(mine, own, zyrows, every, to(dz=3))
    zyz[2] = send(mine, own, zyrows, every, to(dz=2))
    share(mine, own, every, every)

    for zi in KS:
        xz[zi].wait_recv()
        source = whole.at[block_of(zi, 0)]
        x_across(zi, source)
        x_down(zi, 0, source)
        share(source, block_of(zi, 0), xpart, every)
    for zi in (0, 1, 3, 2):
        for k in (1, 3):
            xy[zi, k].wait_recv()
        source = whole.at[block_of(zi, 1)]
        x_down(zi, 1, source)
        share(source, block_of(zi, 1), xpart, every)
    for k in (1, 3):
        zy[k].wait_recv()
    source = whole.at[block_of(0, 1)]
    for k in KS:
        zz[k] = send(source, block_of(0, 1), zrows, every, to(dz=k))
    share(source, block_of(0, 1), zrows, every)
    for zi in KS:
        zyz[zi].wait_recv()
        source = whole.at[block_of(zi, 0)]
        y_across(zi, source)
        share(source, block_of(zi, 0), zyrows, every)
    for zi in (0, 1, 3, 2):
        for k in (1, 3):
            yy[zi, k].wait_recv()
        share(whole.at[block_of(zi, 1)], block_of(zi, 1), yrows, every)
    for zi in KS:
        zz[zi].wait_recv()
        share(whole.at[block_of(zi, 1)], block_of(zi, 1), zrows, every)
    for yi in (0, 1):
        for zi in (0, 1, 3, 2):
            for k in KS if zi or yi else ():
                xx[zi, yi, k].wait_recv()
                rows = pl.ds(pl.multiple_of(GX_PART * flip(x, k), 8), GX_PART)
                share(whole.at[block_of(zi, yi)], block_of(zi, yi), rows, every)
    keep.wait()
    for copy in shared:
        copy.wait_recv()
    for copy in started:
        copy.wait_send()


def gather_blocks(mine):
    rows, features = mine.shape
    copies = 120
    whole = pl.pallas_call(
        gather_kernel,
        out_shape=jax.ShapeDtypeStruct((16, rows, features), mine.dtype),
        in_specs=[pl.BlockSpec(memory_space=pl.ANY)],
        out_specs=pl.BlockSpec(memory_space=pl.ANY),
        scratch_shapes=[
            pltpu.SemaphoreType.DMA(()),
            pltpu.SemaphoreType.DMA((copies,)),
            pltpu.SemaphoreType.DMA((copies,)),
        ],
        compiler_params=pltpu.CompilerParams(collective_id=1, has_side_effects=True),
        name="gather_blocks",
    )(mine)
    return whole.reshape(16 * rows, features)


def per_device(tokens, timesteps, table, weight_values, weight_scales, cotangent):
    moved, factor = modulate(tokens, timesteps, table)
    upstream = cotangent.astype(jnp.float32)
    weight = gather_blocks(dequantize(weight_values, weight_scales))
    preact = jnp.einsum("td,fd->tf", moved, weight, preferred_element_type=jnp.float32)
    gelu_value, derivative = gelu_slope(preact)
    hidden = gelu_value.astype(jnp.bfloat16)
    grad_pre = (upstream * derivative).astype(jnp.bfloat16)
    grad_weight, grad_tokens = reduce_blocks(
        grad_pre, moved, weight, tokens, factor.reshape(factor.shape[0], -1)
    )
    return (hidden, grad_weight, grad_tokens)


def solution(mesh):
    placed = (
        P(("replica", "shard"), None),
        P(("replica", "shard")),
        P(),
        P("shard", None),
        P("shard", None),
        P(("replica", "shard"), None),
    )
    return jax.shard_map(
        per_device,
        mesh=mesh,
        in_specs=placed,
        out_specs=(P(("replica", "shard"), None), P("shard", None), P(("replica", "shard"), None)),
        check_vma=False,
    )
```

```python
import jax
import jax.numpy as jnp
from jax import lax
from jax.experimental import pallas as pl
from jax.experimental.pallas import tpu as pltpu
from jax.sharding import PartitionSpec as P

root_two_over_pi = 0.7978845608028654
cubic_coef = 0.044715
epsilon = 1e-06


def gelu_slope(preact):
    inner_term = root_two_over_pi * (preact + cubic_coef * preact * preact * preact)
    tangent = jnp.tanh(inner_term)
    gelu_value = 0.5 * preact * (1.0 + tangent)
    derivative = 0.5 * (1.0 + tangent) + 0.5 * preact * (
        1.0 - tangent * tangent
    ) * root_two_over_pi * (1.0 + 3.0 * cubic_coef * preact * preact)
    return (gelu_value, derivative)


def dequantize(weight_values, weight_scales):
    row_count, features = weight_values.shape
    blocks = weight_scales.shape[1]
    expanded = (
        weight_values.astype(jnp.float32).reshape(row_count, blocks, features // blocks)
        * weight_scales.astype(jnp.float32)[:, :, None]
    )
    return expanded.reshape(row_count, features).astype(jnp.bfloat16)


def pick(timesteps, table):
    step_count, _, features = table.shape
    onehot = (timesteps[:, None] == jnp.arange(step_count, dtype=jnp.int32)[None, :]).astype(
        jnp.float32
    )
    picked = jnp.dot(
        onehot, table.reshape(step_count, 2 * features), precision=lax.Precision.HIGHEST
    )
    return picked[:, :features], 1.0 + picked[:, features:]


MESH = pl.DeviceIdType.MESH
KS = (1, 3, 2)
Z_ROWS, X_ROWS, Y_ROWS = 112, 96, 96
X_AT, Y_AT = Z_ROWS, Z_ROWS + X_ROWS
OWN_ROWS = Z_ROWS + X_ROWS + Y_ROWS
WINDOWS = ((0, 1024), (1024, 1024), (2048, 1024), (3072, 1024), (4096, 768))


def flip(value, k):
    low, high = value % 2, value // 2
    if k & 1:
        low = 1 - low
    if k & 2:
        high = 1 - high
    return 2 * high + low


def place():
    replica, shard = lax.axis_index("replica"), lax.axis_index("shard")
    return (replica // 2, 2 * (replica % 2) + (shard // 2) % 2, shard // 4, shard % 2)


def device_at(x, y, z, core):
    return (2 * x + y // 2, (2 * z + y % 2) * 2 + core)


def quarter(x):
    return pl.multiple_of(jnp.minimum(512 * x, 1408), 128)


def half(y):
    return pl.multiple_of(896 * (y // 2), 128)


def part(v):
    return pl.multiple_of(256 * v, 128)


def add_rows(rows, store, loads):
    def body(step, _):
        at = pl.ds(pl.multiple_of(step * 16, 16), 16)
        total = loads[0](at).astype(jnp.float32)
        for load in loads[1:]:
            total = total + load(at).astype(jnp.float32)
        store(at, total)
        return 0

    lax.fori_loop(0, rows // 16, body, 0)


def reduce_kernel(
    gradient_rows, gradient, moved, weight, tokens, factor, out, grad_tokens, grad_moved, own, operand, tokens_all,
    weight_parts, gradient_parts, zr1, zr2, zr3, xr1, xr2, xr3, yr1, yr2, yr3,
    zb, zc, xb, xc, yb, yc, pieces, local_sem, core_sem, part_sem, s1, r1, s2, r2, s3, r3, s4, r4,
):
    x, y, z, core = place()

    def to(dx=0, dy=0, dz=0, dc=0):
        return device_at(flip(x, dx), flip(y, dy), flip(z, dz), 1 - core if dc else core)

    peers = [to(dc=1)]
    peers += [to(dx=k) for k in KS] + [to(dy=k) for k in KS] + [to(dz=k) for k in KS]
    barrier = pltpu.get_barrier_semaphore()
    for peer in peers:
        pl.semaphore_signal(barrier, inc=1, device_id=peer, device_id_type=MESH)
    pl.semaphore_wait(barrier, len(peers))

    started = []

    def send(src, dst, send_sem, recv_sem, peer):
        copy = pltpu.make_async_remote_copy(
            src_ref=src, dst_ref=dst, send_sem=send_sem, recv_sem=recv_sem,
            device_id=peer, device_id_type=MESH,
        )
        copy.start()
        started.append(copy)
        return copy

    def fetch(w):
        at, size = WINDOWS[w]
        return [
            pltpu.make_async_copy(
                weight.at[pl.ds(at, size), :],
                weight_parts.at[w % 2, pl.ds(0, size), :],
                part_sem.at[0, w % 2],
            ),
            pltpu.make_async_copy(
                gradient.at[:, pl.ds(at, size)],
                gradient_parts.at[w % 2, :, pl.ds(0, size)],
                part_sem.at[1, w % 2],
            ),
        ]

    count = moved.shape[0]
    lanes = pl.ds(pl.multiple_of(core * count, 128), count)
    mine_moved = pltpu.make_async_copy(moved, tokens_all.at[lanes, :], local_sem.at[8])
    mine_moved.start()
    their_moved = send(
        moved, tokens_all.at[lanes, :], core_sem.at[0, 8], core_sem.at[1, 8], to(dc=1)
    )
    swaps = {}
    order = [(zi, yi) for zi in (1, 3, 2, 0) for yi in (1, 0)]
    for n, (zi, yi) in enumerate(order):
        block = 2 * flip(z, zi) + flip(y, yi) % 2
        mine = pltpu.make_async_copy(
            gradient_rows.at[2 * block + core], operand.at[zi, yi, :, lanes], local_sem.at[n]
        )
        mine.start()
        theirs = send(
            gradient_rows.at[2 * block + 1 - core], operand.at[zi, yi, :, lanes],
            core_sem.at[0, n], core_sem.at[1, n], to(dc=1),
        )
        swaps[zi, yi] = (mine, theirs)
    windows = [fetch(0), fetch(1)]
    for pair in windows:
        for copy in pair:
            copy.start()
    mine_moved.wait()
    their_moved.wait_recv()

    first = {"z": [], "x": [], "y": []}
    for zi, yi in order:
        if yi:
            for each in (1, 0):
                mine, theirs = swaps[zi, each]
                mine.wait()
                theirs.wait_recv()
            rows = operand[zi].reshape(2 * OWN_ROWS, 2 * count)
            for at, size in ((0, 1024), (1024, 896)):
                term = jnp.dot(
                    rows, tokens_all[:, at : at + size], preferred_element_type=jnp.float32
                )
                own[zi, :, :, at : at + size] = term.astype(jnp.bfloat16).reshape(
                    2, OWN_ROWS, size
                )
        if zi:
            n = (zi - 1) * 2 + yi
            first["z"].append(send(
                own.at[zi, yi, pl.ds(0, Z_ROWS), :], zr1.at[zi - 1, yi],
                s1.at[n], r1.at[n], to(dz=zi),
            ))
        for k in KS:
            n = 6 + (zi * 2 + yi) * 3 + k - 1
            first["x"].append(send(
                own.at[zi, yi, pl.ds(X_AT, X_ROWS), pl.ds(quarter(flip(x, k)), 512)],
                xr1.at[k - 1, zi, yi], s1.at[n], r1.at[n], to(dx=k),
            ))
        for k in (1, 3) if yi else (2,):
            n = 30 + zi * 3 + k - 1
            first["y"].append(send(
                own.at[zi, yi, pl.ds(Y_AT, Y_ROWS), pl.ds(half(flip(y, k)), 1024)],
                yr1.at[k - 1, zi], s1.at[n], r1.at[n], to(dy=k),
            ))

    for w in range(len(WINDOWS)):
        for copy in windows[w]:
            copy.wait()
        size = WINDOWS[w][1]
        for at, width in ((0, 1024), (1024, 896)):
            term = jnp.dot(
                gradient_parts[w % 2, :, 0:size],
                weight_parts[w % 2, 0:size, at : at + width],
                preferred_element_type=jnp.float32,
            )
            columns = slice(at, at + width)
            grad_moved[:, columns] = term if w == 0 else grad_moved[:, columns] + term
        if w + 2 < len(WINDOWS):
            windows.append(fetch(w + 2))
            for copy in windows[w + 2]:
                copy.start()

    def store_to(ref):
        def store(at, total):
            ref[at, :] = total.astype(jnp.bfloat16)

        return store

    def shifted(ref, base, columns):
        return lambda at: ref[pl.ds(base + at.start, at.size), columns]

    def plain(ref):
        return lambda at: ref[at, :]

    second = {"z": [], "x": [], "y": []}
    for copy in first["z"]:
        copy.wait_recv()
    for yi in (0, 1):
        add_rows(
            Z_ROWS, store_to(zb.at[yi]),
            [plain(own.at[0, yi])] + [plain(zr1.at[k - 1, yi]) for k in KS],
        )
    for k in KS:
        second["z"].append(send(
            zb.at[:, :, pl.ds(quarter(flip(x, k)), 512)], zr2.at[k - 1],
            s2.at[k - 1], r2.at[k - 1], to(dx=k),
        ))
    for copy in first["y"]:
        copy.wait_recv()
    for zi in (1, 3, 2, 0):
        columns = pl.ds(half(y), 1024)
        add_rows(
            Y_ROWS, store_to(yb.at[zi]),
            [shifted(own.at[zi, 0], Y_AT, columns)] + [plain(yr1.at[k - 1, zi]) for k in KS],
        )
        if zi:
            second["y"].append(send(
                yb.at[zi], yr2.at[zi - 1], s2.at[2 + zi], r2.at[2 + zi], to(dz=zi)
            ))
    for copy in first["x"]:
        copy.wait_recv()
    for yi in (1, 0):
        for zi in range(4):
            columns = pl.ds(quarter(x), 512)
            add_rows(
                X_ROWS, store_to(xb.at[zi, yi]),
                [shifted(own.at[zi, yi], X_AT, columns)]
                + [plain(xr1.at[k - 1, zi, yi]) for k in KS],
            )
        for k in (1, 3) if yi else (2,):
            second["x"].append(send(
                xb.at[:, yi, :, pl.ds(part(flip(y, k) // 2), 256)], xr2.at[k - 1],
                s2.at[5 + k], r2.at[5 + k], to(dy=k),
            ))

    per_sample = count // factor.shape[0]

    def finish(step, _):
        at = pl.ds(pl.multiple_of(step * 16, 16), 16)
        value = tokens[at, :].astype(jnp.float32)
        centre = value - jnp.mean(value, axis=1, keepdims=True)
        inverse = lax.rsqrt(jnp.mean(centre * centre, axis=1, keepdims=True) + epsilon)
        normed = centre * inverse
        scaled_grad = grad_moved[at, :] * factor[pl.ds(step * 16 // per_sample, 1), :]
        mean_grad = jnp.mean(scaled_grad, axis=1, keepdims=True)
        mean_prod = jnp.mean(scaled_grad * normed, axis=1, keepdims=True)
        result = inverse * (scaled_grad - mean_grad - normed * mean_prod)
        grad_tokens[at, :] = result.astype(jnp.bfloat16)
        return 0

    lax.fori_loop(0, count // 16, finish, 0)

    third = {"z": [], "x": [], "y": []}
    for copy in second["z"]:
        copy.wait_recv()
    for yi in (1, 0):
        columns = pl.ds(quarter(x), 512)
        add_rows(
            Z_ROWS, store_to(zc.at[yi]),
            [shifted(zb.at[yi], 0, columns)] + [plain(zr2.at[k - 1, yi]) for k in KS],
        )
        for k in (1, 3) if yi else (2,):
            third["z"].append(send(
                zc.at[yi, :, pl.ds(part(flip(y, k) // 2), 256)], zr3.at[k - 1],
                s3.at[k - 1], r3.at[k - 1], to(dy=k),
            ))
    for copy in second["y"]:
        copy.wait_recv()
    add_rows(Y_ROWS, store_to(yc), [plain(yb.at[0])] + [plain(yr2.at[k - 1]) for k in KS])
    for k in KS:
        third["y"].append(send(
            yc.at[:, pl.ds(part(flip(x, k)), 256)], yr3.at[k - 1],
            s3.at[2 + k], r3.at[2 + k], to(dx=k),
        ))
    for copy in second["x"]:
        copy.wait_recv()
    for zi in (1, 3, 2, 0):
        columns = pl.ds(part(y // 2), 256)
        add_rows(
            X_ROWS, store_to(xc.at[zi]),
            [shifted(xb.at[zi, 0], 0, columns)] + [plain(xr2.at[k - 1, zi]) for k in KS],
        )
        if zi:
            third["x"].append(send(
                xc.at[zi], xr3.at[zi - 1], s3.at[5 + zi], r3.at[5 + zi], to(dz=zi)
            ))

    def store_piece(base):
        def store(at, total):
            pieces[0, pl.ds(base + at.start, at.size), :] = total.astype(jnp.bfloat16)

        return store

    for copy in third["z"]:
        copy.wait_recv()
    columns = pl.ds(part(y // 2), 256)
    add_rows(
        Z_ROWS, store_piece(0),
        [shifted(zc.at[0], 0, columns)] + [plain(zr3.at[k - 1]) for k in KS],
    )
    for copy in third["y"]:
        copy.wait_recv()
    own_columns = pl.ds(part(x), 256)
    add_rows(
        Y_ROWS, store_piece(Y_AT),
        [shifted(yc, 0, own_columns)] + [plain(yr3.at[k - 1]) for k in KS],
    )
    for copy in third["x"]:
        copy.wait_recv()
    add_rows(
        X_ROWS, store_piece(X_AT), [plain(xc.at[0])] + [plain(xr3.at[k - 1]) for k in KS]
    )

    def hand(source, slot, peer):
        return send(
            pieces.at[source], pieces.at[slot], s4.at[slot - 1], r4.at[slot - 1], peer
        )

    along = {k: hand(0, 2 * k, to(dx=k)) for k in KS}
    across = [hand(0, 1, to(dy=2))]
    for k in KS:
        along[k].wait_recv()
        across.append(hand(2 * k, 2 * k + 1, to(dy=2)))
    for copy in across:
        copy.wait_recv()
    for px in range(4):
        for ph in range(2):
            lows = (px % 2 + x % 2) % 2
            highs = (px // 2 + x // 2) % 2
            slot = 2 * (2 * highs + lows) + (ph + y // 2) % 2
            at = min(512 * px, 1408) + 256 * ph
            out[0:Y_AT, at : at + 256] = pieces[slot, 0:Y_AT, :].astype(jnp.float32)
    for ph in range(2):
        for px in range(4):
            lows = (px % 2 + x % 2) % 2
            highs = (px // 2 + x // 2) % 2
            slot = 2 * (2 * highs + lows) + (ph + y // 2) % 2
            at = 896 * ph + 256 * px
            out[Y_AT:OWN_ROWS, at : at + 256] = pieces[slot, Y_AT:OWN_ROWS, :].astype(jnp.float32)
    for copy in started:
        copy.wait_send()


def reduce_blocks(gradient_rows, grad_pre, moved, weight, tokens, factor):
    count, features = moved.shape
    bf16 = jnp.bfloat16
    shapes = [
        (4, 2, OWN_ROWS, features), (4, 2, OWN_ROWS, 2 * count), (2 * count, features),
        (2, 1024, features), (2, count, 1024),
        (3, 2, Z_ROWS, features), (3, 2, Z_ROWS, 512), (3, Z_ROWS, 256),
        (3, 4, 2, X_ROWS, 512), (3, 4, X_ROWS, 256), (3, X_ROWS, 256),
        (3, 4, Y_ROWS, 1024), (3, Y_ROWS, 1024), (3, Y_ROWS, 256),
        (2, Z_ROWS, features), (2, Z_ROWS, 512),
        (4, 2, X_ROWS, 512), (4, X_ROWS, 256),
        (4, Y_ROWS, 1024), (Y_ROWS, 1024),
        (8, OWN_ROWS, 256),
    ]
    sems = [(9,), (2, 9), (2, 2), (42,), (42,), (9,), (9,), (9,), (9,), (7,), (7,)]
    return pl.pallas_call(
        reduce_kernel,
        out_shape=(
            jax.ShapeDtypeStruct((OWN_ROWS, features), jnp.float32),
            jax.ShapeDtypeStruct((count, features), bf16),
        ),
        in_specs=[pl.BlockSpec(memory_space=pl.ANY)] * 4
        + [pl.BlockSpec(memory_space=pltpu.VMEM)] * 2,
        out_specs=[pl.BlockSpec(memory_space=pltpu.VMEM)] * 2,
        scratch_shapes=[pltpu.VMEM((count, features), jnp.float32)]
        + [pltpu.VMEM(shape, bf16) for shape in shapes]
        + [pltpu.SemaphoreType.DMA(shape) for shape in sems],
        compiler_params=pltpu.CompilerParams(
            collective_id=0, has_side_effects=True, vmem_limit_bytes=60 << 20
        ),
        name="reduce_blocks",
    )(gradient_rows.reshape(-1, OWN_ROWS, count), grad_pre, moved, weight, tokens, factor)


GX_ROWS, GZ_ROWS, GY_ROWS = 128, 32, 144
GX_PART = GX_ROWS // 4
GY_AT = GX_ROWS + GZ_ROWS
HALVES = {1: (0, 1024), 3: (1024, 896)}
TILE = 128
NEAR, FAR = 9, 10
CHUNK = 256


def forward_kernel(
    mine, tokens, shift, factor, cotangent,
    whole_out, hidden, gradient, gradient_rows, moved,
    whole, upstream, hidden_part, gradient_part, rows_part,
    own_sem, ss, rs, up_sem, out_sem, whole_sem,
):
    x, y, z, core = place()

    def to(dx=0, dy=0, dz=0, dc=0):
        return device_at(flip(x, dx), flip(y, dy), flip(z, dz), 1 - core if dc else core)

    peers = [to(dc=1)]
    peers += [to(dx=k) for k in KS] + [to(dy=k) for k in (1, 3)] + [to(dz=k) for k in KS]
    barrier = pltpu.get_barrier_semaphore()
    for peer in peers:
        pl.semaphore_signal(barrier, inc=1, device_id=peer, device_id_type=MESH)
    pl.semaphore_wait(barrier, len(peers))

    started = []

    def block_of(zi, yi):
        return 2 * (2 * flip(z, zi) + flip(y, yi) % 2) + core

    blocks = {(zi, yi): block_of(zi, yi) for zi in range(4) for yi in (0, 1)}
    own = blocks[0, 0]
    height = mine.shape[0]

    def within(block, rows):
        return pl.ds(pl.multiple_of(height * block + rows[0], 16), rows[1])

    def send(block, rows, columns, peer):
        n = len(started)
        if block is own:
            source = mine.at[pl.ds(*rows), columns]
        else:
            source = whole.at[within(block, rows), columns]
        copy = pltpu.make_async_remote_copy(
            src_ref=source,
            dst_ref=whole.at[within(block, rows), columns],
            send_sem=ss.at[n], recv_sem=rs.at[n],
            device_id=peer, device_id_type=MESH,
        )
        copy.start()
        started.append(copy)
        return copy

    every = slice(None)
    keep = pltpu.make_async_copy(mine, whole.at[within(own, (0, height)), :], own_sem)
    keep.start()
    shared = {0: [], 1: [], 3: [], 2: []}

    def share(zi, yi, rows):
        shared[zi].append(send(blocks[zi, yi], rows, every, to(dc=1)))

    xpart = (GX_PART * x, GX_PART)
    zrows, yrows = (GX_ROWS, GZ_ROWS), (GY_AT, GY_ROWS)
    zyrows = (GX_ROWS, GZ_ROWS + GY_ROWS)
    cols = {k: pl.ds(*HALVES[k]) for k in HALVES}
    xz, xy, xx, zyz, yy, zy, zz = {}, {}, {}, {}, {}, {}, {}

    def x_down(zi, yi):
        for k in KS:
            xx[zi, yi, k] = send(blocks[zi, yi], xpart, every, to(dx=k))
        share(zi, yi, xpart)

    def x_across(zi):
        for k in (1, 3):
            xy[zi, k] = send(blocks[zi, 0], xpart, cols[k], to(dy=k))

    def y_across(zi):
        for k in (1, 3):
            yy[zi, k] = send(blocks[zi, 0], yrows, cols[k], to(dy=k))

    def received(*copies):
        for copy in copies:
            copy.wait_recv()

    for k in KS:
        xz[k] = send(own, xpart, every, to(dz=k))
    x_across(0)
    for k in (1, 3):
        zy[k] = send(own, zrows, cols[k], to(dy=k))
    zyz[1] = send(own, zyrows, every, to(dz=1))
    share(0, 0, (0, height))
    for zi in KS:
        received(xz[zi])
        x_across(zi)
    y_across(0)
    received(xy[0, 1], xy[0, 3])
    x_down(0, 1)
    received(zy[1], zy[3])
    zz[1] = send(blocks[0, 1], zrows, every, to(dz=1))
    share(0, 1, zrows)
    for k in (3, 2):
        zyz[k] = send(own, zyrows, every, to(dz=k))
        zz[k] = send(blocks[0, 1], zrows, every, to(dz=k))
    for zi in KS:
        x_down(zi, 0)
        received(xy[zi, 1], xy[zi, 3])
        x_down(zi, 1)

    count = tokens.shape[0]
    per_sample = count // factor.shape[0]

    def normalize(step, _):
        at = pl.ds(pl.multiple_of(step * 16, 16), 16)
        value = tokens[at, :].astype(jnp.float32)
        centre = value - jnp.mean(value, axis=1, keepdims=True)
        inverse = lax.rsqrt(jnp.mean(centre * centre, axis=1, keepdims=True) + epsilon)
        sample = pl.ds(step * 16 // per_sample, 1)
        moved[at, :] = (centre * inverse * factor[sample, :] + shift[sample, :]).astype(
            jnp.bfloat16
        )
        return 0

    lax.fori_loop(0, count // 16, normalize, 0)

    low = z % 2
    plan = []
    for zi, tiles in ((0, NEAR), (1, FAR), (3, NEAR), (2, FAR)):
        high = flip(z, zi) % 2
        first = 19 * (flip(z, zi) // 2) + high * (19 - tiles)
        plan.append((zi, tiles * TILE, pl.multiple_of(first * TILE, TILE)))

    def fetch(n):
        zi, size, at = plan[n]
        copy = pltpu.make_async_copy(
            cotangent.at[:, pl.ds(at, size)],
            upstream.at[n % 2, :, pl.ds(0, size)],
            up_sem.at[n % 2],
        )
        copy.start()
        return copy

    fetched = [fetch(0), fetch(1)]
    stores = []
    saved = []

    def window(n):
        zi, size, at = plan[n]
        slot = n % 2
        fetched[n].wait()
        if n >= 2:
            for copy in stores[n - 2]:
                copy.wait()

        def piece(begin, width):
            values = whole[pl.ds(pl.multiple_of(at + begin, TILE), width), :]
            preact = lax.dot_general(
                moved[...], values, (((1,), (1,)), ((), ())),
                preferred_element_type=jnp.float32,
            )
            gelu_value, derivative = gelu_slope(preact)
            columns = pl.ds(begin, width)
            hidden_part[slot, :, columns] = gelu_value.astype(jnp.bfloat16)
            grad = (upstream[slot, :, columns].astype(jnp.float32) * derivative).astype(
                jnp.bfloat16
            )
            gradient_part[slot, :, columns] = grad
            rows_part[slot, columns, :] = grad.T

        def step(i, _):
            piece(pl.multiple_of(i * CHUNK, CHUNK), CHUNK)
            return 0

        lax.fori_loop(0, size // CHUNK, step, 0)
        if size % CHUNK:
            piece(size - size % CHUNK, size % CHUNK)
        target = pl.ds(at, size)
        copies = [
            pltpu.make_async_copy(
                hidden_part.at[slot, :, pl.ds(0, size)], hidden.at[:, target], out_sem.at[0, slot]
            ),
            pltpu.make_async_copy(
                gradient_part.at[slot, :, pl.ds(0, size)], gradient.at[:, target],
                out_sem.at[1, slot],
            ),
            pltpu.make_async_copy(
                rows_part.at[slot, pl.ds(0, size), :], gradient_rows.at[target, :],
                out_sem.at[2, slot],
            ),
        ]
        for copy in copies:
            copy.start()
        stores.append(copies)
        if n + 2 < len(plan):
            fetched.append(fetch(n + 2))

    def land(zi):
        if zi:
            received(zz[zi])
            share(zi, 1, zrows)
        received(yy[zi, 1], yy[zi, 3])
        share(zi, 1, yrows)
        for yi in (0, 1):
            for k in KS if zi or yi else ():
                received(xx[zi, yi, k])
                share(zi, yi, (GX_PART * flip(x, k), GX_PART))
        received(*shared[zi])
        landed = within(4 * flip(z, zi), (0, 4 * height))
        copy = pltpu.make_async_copy(
            whole.at[landed, :], whole_out.at[landed, :], whole_sem.at[zi]
        )
        copy.start()
        saved.append(copy)

    def relay(zi):
        received(zyz[zi])
        y_across(zi)
        share(zi, 0, zyrows)

    keep.wait()
    relay(1)
    land(0)
    window(0)
    relay(3)
    land(1)
    window(1)
    land(3)
    relay(2)
    window(2)
    land(2)
    window(3)
    for copies in stores[2:]:
        for copy in copies:
            copy.wait()
    for copy in saved:
        copy.wait()
    for copy in started:
        copy.wait_send()


def forward_blocks(mine, tokens, shift, factor, cotangent):
    rows, features = mine.shape
    count, units = cotangent.shape
    copies, widest = 120, FAR * TILE
    bf16 = jnp.bfloat16
    vmem = pl.BlockSpec(memory_space=pltpu.VMEM)
    anywhere = pl.BlockSpec(memory_space=pl.ANY)
    return pl.pallas_call(
        forward_kernel,
        out_shape=(
            jax.ShapeDtypeStruct((16 * rows, features), bf16),
            jax.ShapeDtypeStruct((count, units), bf16),
            jax.ShapeDtypeStruct((count, units), bf16),
            jax.ShapeDtypeStruct((units, count), bf16),
            jax.ShapeDtypeStruct((count, features), bf16),
        ),
        in_specs=[vmem, vmem, vmem, vmem, anywhere],
        out_specs=(anywhere, anywhere, anywhere, anywhere, vmem),
        scratch_shapes=[
            pltpu.VMEM((16 * rows, features), bf16),
            pltpu.VMEM((2, count, widest), bf16),
            pltpu.VMEM((2, count, widest), bf16),
            pltpu.VMEM((2, count, widest), bf16),
            pltpu.VMEM((2, widest, count), bf16),
            pltpu.SemaphoreType.DMA(()),
            pltpu.SemaphoreType.DMA((copies,)),
            pltpu.SemaphoreType.DMA((copies,)),
            pltpu.SemaphoreType.DMA((2,)),
            pltpu.SemaphoreType.DMA((3, 2)),
            pltpu.SemaphoreType.DMA((4,)),
        ],
        compiler_params=pltpu.CompilerParams(
            collective_id=1, has_side_effects=True, vmem_limit_bytes=60 << 20
        ),
        name="forward_blocks",
    )(mine, tokens, shift, factor, cotangent)


def per_device(tokens, timesteps, table, weight_values, weight_scales, cotangent):
    shift, factor = pick(timesteps, table)
    weight, hidden, grad_pre, gradient_rows, moved = forward_blocks(
        dequantize(weight_values, weight_scales), tokens, shift, factor, cotangent
    )
    grad_weight, grad_tokens = reduce_blocks(
        gradient_rows, grad_pre, moved, weight, tokens, factor
    )
    return (hidden, grad_weight, grad_tokens)


def solution(mesh):
    placed = (
        P(("replica", "shard"), None),
        P(("replica", "shard")),
        P(),
        P("shard", None),
        P("shard", None),
        P(("replica", "shard"), None),
    )
    return jax.shard_map(
        per_device,
        mesh=mesh,
        in_specs=placed,
        out_specs=(P(("replica", "shard"), None), P("shard", None), P(("replica", "shard"), None)),
        check_vma=False,
    )
```

```python
import jax
import jax.numpy as jnp
from jax import lax
from jax.experimental import pallas as pl
from jax.experimental.pallas import tpu as pltpu
from jax.sharding import PartitionSpec as P

root_two_over_pi = 0.7978845608028654
cubic_coef = 0.044715
epsilon = 1e-06


def gelu_slope(preact):
    inner_term = root_two_over_pi * (preact + cubic_coef * preact * preact * preact)
    tangent = jnp.tanh(inner_term)
    gelu_value = 0.5 * preact * (1.0 + tangent)
    derivative = 0.5 * (1.0 + tangent) + 0.5 * preact * (
        1.0 - tangent * tangent
    ) * root_two_over_pi * (1.0 + 3.0 * cubic_coef * preact * preact)
    return (gelu_value, derivative)


def dequantize(weight_values, weight_scales):
    row_count, features = weight_values.shape
    blocks = weight_scales.shape[1]
    expanded = (
        weight_values.astype(jnp.float32).reshape(row_count, blocks, features // blocks)
        * weight_scales.astype(jnp.float32)[:, :, None]
    )
    return expanded.reshape(row_count, features).astype(jnp.bfloat16)


def pick(timesteps, table):
    step_count, _, features = table.shape
    onehot = (timesteps[:, None] == jnp.arange(step_count, dtype=jnp.int32)[None, :]).astype(
        jnp.float32
    )
    picked = jnp.dot(
        onehot, table.reshape(step_count, 2 * features), precision=lax.Precision.HIGHEST
    )
    return picked[:, :features], 1.0 + picked[:, features:]


MESH = pl.DeviceIdType.MESH
KS = (1, 3, 2)
Z_ROWS, X_ROWS, Y_ROWS = 96, 96, 112
X_AT, Y_AT = Z_ROWS, Z_ROWS + X_ROWS
OWN_ROWS = Z_ROWS + X_ROWS + Y_ROWS
WINDOWS = ((0, 1024), (1024, 1024), (2048, 1024), (3072, 1024), (4096, 768))


def flip(value, k):
    low, high = value % 2, value // 2
    if k & 1:
        low = 1 - low
    if k & 2:
        high = 1 - high
    return 2 * high + low


def place():
    replica, shard = lax.axis_index("replica"), lax.axis_index("shard")
    return (replica // 2, 2 * (replica % 2) + (shard // 2) % 2, shard // 4, shard % 2)


def device_at(x, y, z, core):
    return (2 * x + y // 2, (2 * z + y % 2) * 2 + core)


def quarter(x):
    return pl.multiple_of(jnp.minimum(512 * x, 1408), 128)


def half(y):
    return pl.multiple_of(896 * (y // 2), 128)


def part(v):
    return pl.multiple_of(256 * v, 128)


def add_rows(rows, store, loads):
    def body(step, _):
        at = pl.ds(pl.multiple_of(step * 16, 16), 16)
        total = loads[0](at).astype(jnp.float32)
        for load in loads[1:]:
            total = total + load(at).astype(jnp.float32)
        store(at, total)
        return 0

    lax.fori_loop(0, rows // 16, body, 0)


def reduce_kernel(
    gradient_rows, gradient, moved, weight, tokens, factor, out, grad_tokens, grad_moved, own, operand, tokens_all,
    weight_parts, gradient_parts, zr1, zr2, zr3, xr1, xr2, xr3, yr1, yr2, yr3,
    zb, zc, xb, xc, yb, yc, pieces, local_sem, core_sem, part_sem, s1, r1, s2, r2, s3, r3, s4, r4,
):
    x, y, z, core = place()

    def to(dx=0, dy=0, dz=0, dc=0):
        return device_at(flip(x, dx), flip(y, dy), flip(z, dz), 1 - core if dc else core)

    peers = [to(dc=1)]
    peers += [to(dx=k) for k in KS] + [to(dy=k) for k in KS] + [to(dz=k) for k in KS]
    barrier = pltpu.get_barrier_semaphore()
    for peer in peers:
        pl.semaphore_signal(barrier, inc=1, device_id=peer, device_id_type=MESH)
    pl.semaphore_wait(barrier, len(peers))

    started = []

    def send(src, dst, send_sem, recv_sem, peer):
        copy = pltpu.make_async_remote_copy(
            src_ref=src, dst_ref=dst, send_sem=send_sem, recv_sem=recv_sem,
            device_id=peer, device_id_type=MESH,
        )
        copy.start()
        started.append(copy)
        return copy

    def fetch(w):
        at, size = WINDOWS[w]
        return [
            pltpu.make_async_copy(
                weight.at[pl.ds(at, size), :],
                weight_parts.at[w % 2, pl.ds(0, size), :],
                part_sem.at[0, w % 2],
            ),
            pltpu.make_async_copy(
                gradient.at[:, pl.ds(at, size)],
                gradient_parts.at[w % 2, :, pl.ds(0, size)],
                part_sem.at[1, w % 2],
            ),
        ]

    count = moved.shape[0]
    lanes = pl.ds(pl.multiple_of(core * count, 128), count)
    mine_moved = pltpu.make_async_copy(moved, tokens_all.at[lanes, :], local_sem.at[8])
    mine_moved.start()
    their_moved = send(
        moved, tokens_all.at[lanes, :], core_sem.at[0, 8], core_sem.at[1, 8], to(dc=1)
    )
    swaps = {}
    order = [(zi, yi) for zi in (1, 3, 2, 0) for yi in (1, 0)]
    for n, (zi, yi) in enumerate(order):
        block = 2 * flip(z, zi) + flip(y, yi) % 2
        mine = pltpu.make_async_copy(
            gradient_rows.at[2 * block + core], operand.at[zi, yi, :, lanes], local_sem.at[n]
        )
        mine.start()
        theirs = send(
            gradient_rows.at[2 * block + 1 - core], operand.at[zi, yi, :, lanes],
            core_sem.at[0, n], core_sem.at[1, n], to(dc=1),
        )
        swaps[zi, yi] = (mine, theirs)
    windows = [fetch(0), fetch(1)]
    for pair in windows:
        for copy in pair:
            copy.start()
    mine_moved.wait()
    their_moved.wait_recv()

    first = {"z": [], "x": [], "y": []}
    for zi, yi in order:
        if yi:
            for each in (1, 0):
                mine, theirs = swaps[zi, each]
                mine.wait()
                theirs.wait_recv()
            rows = operand[zi].reshape(2 * OWN_ROWS, 2 * count)
            for at, size in ((0, 1024), (1024, 896)):
                term = jnp.dot(
                    rows, tokens_all[:, at : at + size], preferred_element_type=jnp.float32
                )
                own[zi, :, :, at : at + size] = term.astype(jnp.bfloat16).reshape(
                    2, OWN_ROWS, size
                )
        if zi:
            n = (zi - 1) * 2 + yi
            first["z"].append(send(
                own.at[zi, yi, pl.ds(0, Z_ROWS), :], zr1.at[zi - 1, yi],
                s1.at[n], r1.at[n], to(dz=zi),
            ))
        for k in KS:
            n = 6 + (zi * 2 + yi) * 3 + k - 1
            first["x"].append(send(
                own.at[zi, yi, pl.ds(X_AT, X_ROWS), pl.ds(quarter(flip(x, k)), 512)],
                xr1.at[k - 1, zi, yi], s1.at[n], r1.at[n], to(dx=k),
            ))
        for k in (1, 3) if yi else (2,):
            n = 30 + zi * 3 + k - 1
            first["y"].append(send(
                own.at[zi, yi, pl.ds(Y_AT, Y_ROWS), pl.ds(half(flip(y, k)), 1024)],
                yr1.at[k - 1, zi], s1.at[n], r1.at[n], to(dy=k),
            ))

    for w in range(len(WINDOWS)):
        for copy in windows[w]:
            copy.wait()
        size = WINDOWS[w][1]
        for at, width in ((0, 1024), (1024, 896)):
            term = jnp.dot(
                gradient_parts[w % 2, :, 0:size],
                weight_parts[w % 2, 0:size, at : at + width],
                preferred_element_type=jnp.float32,
            )
            columns = slice(at, at + width)
            grad_moved[:, columns] = term if w == 0 else grad_moved[:, columns] + term
        if w + 2 < len(WINDOWS):
            windows.append(fetch(w + 2))
            for copy in windows[w + 2]:
                copy.start()

    def store_to(ref):
        def store(at, total):
            ref[at, :] = total.astype(jnp.bfloat16)

        return store

    def shifted(ref, base, columns):
        return lambda at: ref[pl.ds(base + at.start, at.size), columns]

    def plain(ref):
        return lambda at: ref[at, :]

    second = {"z": [], "x": [], "y": []}
    for copy in first["z"]:
        copy.wait_recv()
    for yi in (0, 1):
        add_rows(
            Z_ROWS, store_to(zb.at[yi]),
            [plain(own.at[0, yi])] + [plain(zr1.at[k - 1, yi]) for k in KS],
        )
    for k in KS:
        second["z"].append(send(
            zb.at[:, :, pl.ds(quarter(flip(x, k)), 512)], zr2.at[k - 1],
            s2.at[k - 1], r2.at[k - 1], to(dx=k),
        ))
    for copy in first["y"]:
        copy.wait_recv()
    for zi in (1, 3, 2, 0):
        columns = pl.ds(half(y), 1024)
        add_rows(
            Y_ROWS, store_to(yb.at[zi]),
            [shifted(own.at[zi, 0], Y_AT, columns)] + [plain(yr1.at[k - 1, zi]) for k in KS],
        )
        if zi:
            second["y"].append(send(
                yb.at[zi], yr2.at[zi - 1], s2.at[2 + zi], r2.at[2 + zi], to(dz=zi)
            ))
    for copy in first["x"]:
        copy.wait_recv()
    for yi in (1, 0):
        for zi in range(4):
            columns = pl.ds(quarter(x), 512)
            add_rows(
                X_ROWS, store_to(xb.at[zi, yi]),
                [shifted(own.at[zi, yi], X_AT, columns)]
                + [plain(xr1.at[k - 1, zi, yi]) for k in KS],
            )
        for k in (1, 3) if yi else (2,):
            second["x"].append(send(
                xb.at[:, yi, :, pl.ds(part(flip(y, k) // 2), 256)], xr2.at[k - 1],
                s2.at[5 + k], r2.at[5 + k], to(dy=k),
            ))

    per_sample = count // factor.shape[0]

    def finish(step, _):
        at = pl.ds(pl.multiple_of(step * 16, 16), 16)
        value = tokens[at, :].astype(jnp.float32)
        centre = value - jnp.mean(value, axis=1, keepdims=True)
        inverse = lax.rsqrt(jnp.mean(centre * centre, axis=1, keepdims=True) + epsilon)
        normed = centre * inverse
        scaled_grad = grad_moved[at, :] * factor[pl.ds(step * 16 // per_sample, 1), :]
        mean_grad = jnp.mean(scaled_grad, axis=1, keepdims=True)
        mean_prod = jnp.mean(scaled_grad * normed, axis=1, keepdims=True)
        result = inverse * (scaled_grad - mean_grad - normed * mean_prod)
        grad_tokens[at, :] = result.astype(jnp.bfloat16)
        return 0

    lax.fori_loop(0, count // 16, finish, 0)

    third = {"z": [], "x": [], "y": []}
    for copy in second["z"]:
        copy.wait_recv()
    for yi in (1, 0):
        columns = pl.ds(quarter(x), 512)
        add_rows(
            Z_ROWS, store_to(zc.at[yi]),
            [shifted(zb.at[yi], 0, columns)] + [plain(zr2.at[k - 1, yi]) for k in KS],
        )
        for k in (1, 3) if yi else (2,):
            third["z"].append(send(
                zc.at[yi, :, pl.ds(part(flip(y, k) // 2), 256)], zr3.at[k - 1],
                s3.at[k - 1], r3.at[k - 1], to(dy=k),
            ))
    for copy in second["y"]:
        copy.wait_recv()
    add_rows(Y_ROWS, store_to(yc), [plain(yb.at[0])] + [plain(yr2.at[k - 1]) for k in KS])
    for k in KS:
        third["y"].append(send(
            yc.at[:, pl.ds(part(flip(x, k)), 256)], yr3.at[k - 1],
            s3.at[2 + k], r3.at[2 + k], to(dx=k),
        ))
    for copy in second["x"]:
        copy.wait_recv()
    for zi in (1, 3, 2, 0):
        columns = pl.ds(part(y // 2), 256)
        add_rows(
            X_ROWS, store_to(xc.at[zi]),
            [shifted(xb.at[zi, 0], 0, columns)] + [plain(xr2.at[k - 1, zi]) for k in KS],
        )
        if zi:
            third["x"].append(send(
                xc.at[zi], xr3.at[zi - 1], s3.at[5 + zi], r3.at[5 + zi], to(dz=zi)
            ))

    def store_piece(base):
        def store(at, total):
            pieces[0, pl.ds(base + at.start, at.size), :] = total.astype(jnp.bfloat16)

        return store

    for copy in third["z"]:
        copy.wait_recv()
    columns = pl.ds(part(y // 2), 256)
    add_rows(
        Z_ROWS, store_piece(0),
        [shifted(zc.at[0], 0, columns)] + [plain(zr3.at[k - 1]) for k in KS],
    )
    for copy in third["y"]:
        copy.wait_recv()
    own_columns = pl.ds(part(x), 256)
    add_rows(
        Y_ROWS, store_piece(Y_AT),
        [shifted(yc, 0, own_columns)] + [plain(yr3.at[k - 1]) for k in KS],
    )
    for copy in third["x"]:
        copy.wait_recv()
    add_rows(
        X_ROWS, store_piece(X_AT), [plain(xc.at[0])] + [plain(xr3.at[k - 1]) for k in KS]
    )

    def hand(source, slot, peer):
        return send(
            pieces.at[source], pieces.at[slot], s4.at[slot - 1], r4.at[slot - 1], peer
        )

    along = {k: hand(0, 2 * k, to(dx=k)) for k in KS}
    across = [hand(0, 1, to(dy=2))]
    for k in KS:
        along[k].wait_recv()
        across.append(hand(2 * k, 2 * k + 1, to(dy=2)))
    for copy in across:
        copy.wait_recv()
    for px in range(4):
        for ph in range(2):
            lows = (px % 2 + x % 2) % 2
            highs = (px // 2 + x // 2) % 2
            slot = 2 * (2 * highs + lows) + (ph + y // 2) % 2
            at = min(512 * px, 1408) + 256 * ph
            out[0:Y_AT, at : at + 256] = pieces[slot, 0:Y_AT, :].astype(jnp.float32)
    for ph in range(2):
        for px in range(4):
            lows = (px % 2 + x % 2) % 2
            highs = (px // 2 + x // 2) % 2
            slot = 2 * (2 * highs + lows) + (ph + y // 2) % 2
            at = 896 * ph + 256 * px
            out[Y_AT:OWN_ROWS, at : at + 256] = pieces[slot, Y_AT:OWN_ROWS, :].astype(jnp.float32)
    for copy in started:
        copy.wait_send()


def reduce_blocks(gradient_rows, grad_pre, moved, weight, tokens, factor):
    count, features = moved.shape
    bf16 = jnp.bfloat16
    shapes = [
        (4, 2, OWN_ROWS, features), (4, 2, OWN_ROWS, 2 * count), (2 * count, features),
        (2, 1024, features), (2, count, 1024),
        (3, 2, Z_ROWS, features), (3, 2, Z_ROWS, 512), (3, Z_ROWS, 256),
        (3, 4, 2, X_ROWS, 512), (3, 4, X_ROWS, 256), (3, X_ROWS, 256),
        (3, 4, Y_ROWS, 1024), (3, Y_ROWS, 1024), (3, Y_ROWS, 256),
        (2, Z_ROWS, features), (2, Z_ROWS, 512),
        (4, 2, X_ROWS, 512), (4, X_ROWS, 256),
        (4, Y_ROWS, 1024), (Y_ROWS, 1024),
        (8, OWN_ROWS, 256),
    ]
    sems = [(9,), (2, 9), (2, 2), (42,), (42,), (9,), (9,), (9,), (9,), (7,), (7,)]
    return pl.pallas_call(
        reduce_kernel,
        out_shape=(
            jax.ShapeDtypeStruct((OWN_ROWS, features), jnp.float32),
            jax.ShapeDtypeStruct((count, features), bf16),
        ),
        in_specs=[pl.BlockSpec(memory_space=pl.ANY)] * 4
        + [pl.BlockSpec(memory_space=pltpu.VMEM)] * 2,
        out_specs=[pl.BlockSpec(memory_space=pltpu.VMEM)] * 2,
        scratch_shapes=[pltpu.VMEM((count, features), jnp.float32)]
        + [pltpu.VMEM(shape, bf16) for shape in shapes]
        + [pltpu.SemaphoreType.DMA(shape) for shape in sems],
        compiler_params=pltpu.CompilerParams(
            collective_id=0, has_side_effects=True, vmem_limit_bytes=60 << 20
        ),
        name="reduce_blocks",
    )(gradient_rows.reshape(-1, OWN_ROWS, count), grad_pre, moved, weight, tokens, factor)


GX_ROWS, GZ_ROWS, GY_ROWS = 128, 32, 144
GX_PART = GX_ROWS // 4
GY_AT = GX_ROWS + GZ_ROWS
HALVES = {1: (0, 1024), 3: (1024, 896)}
TILE = 128
NEAR, FAR = 9, 10
CHUNK = 256


def forward_kernel(
    mine, tokens, shift, factor, cotangent,
    whole_out, hidden, gradient, gradient_rows, moved,
    whole, upstream, hidden_part, gradient_part, rows_part,
    own_sem, ss, rs, up_sem, out_sem, whole_sem,
):
    x, y, z, core = place()

    def to(dx=0, dy=0, dz=0, dc=0):
        return device_at(flip(x, dx), flip(y, dy), flip(z, dz), 1 - core if dc else core)

    peers = [to(dc=1)]
    peers += [to(dx=k) for k in KS] + [to(dy=k) for k in (1, 3)] + [to(dz=k) for k in KS]
    barrier = pltpu.get_barrier_semaphore()
    for peer in peers:
        pl.semaphore_signal(barrier, inc=1, device_id=peer, device_id_type=MESH)
    pl.semaphore_wait(barrier, len(peers))

    started = []

    def block_of(zi, yi):
        return 2 * (2 * flip(z, zi) + flip(y, yi) % 2) + core

    blocks = {(zi, yi): block_of(zi, yi) for zi in range(4) for yi in (0, 1)}
    own = blocks[0, 0]
    height = mine.shape[0]

    def within(block, rows):
        return pl.ds(pl.multiple_of(height * block + rows[0], 16), rows[1])

    def send(block, rows, columns, peer):
        n = len(started)
        if block is own:
            source = mine.at[pl.ds(*rows), columns]
        else:
            source = whole.at[within(block, rows), columns]
        copy = pltpu.make_async_remote_copy(
            src_ref=source,
            dst_ref=whole.at[within(block, rows), columns],
            send_sem=ss.at[n], recv_sem=rs.at[n],
            device_id=peer, device_id_type=MESH,
        )
        copy.start()
        started.append(copy)
        return copy

    every = slice(None)
    keep = pltpu.make_async_copy(mine, whole.at[within(own, (0, height)), :], own_sem)
    keep.start()
    shared = {0: [], 1: [], 3: [], 2: []}

    def share(zi, yi, rows):
        shared[zi].append(send(blocks[zi, yi], rows, every, to(dc=1)))

    xpart = (GX_PART * x, GX_PART)
    zrows, yrows = (GX_ROWS, GZ_ROWS), (GY_AT, GY_ROWS)
    zyrows = (GX_ROWS, GZ_ROWS + GY_ROWS)
    cols = {k: pl.ds(*HALVES[k]) for k in HALVES}
    xz, xy, xx, zyz, yy, zy, zz = {}, {}, {}, {}, {}, {}, {}

    def x_down(zi, yi):
        for k in KS:
            xx[zi, yi, k] = send(blocks[zi, yi], xpart, every, to(dx=k))
        share(zi, yi, xpart)

    def x_across(zi):
        for k in (1, 3):
            xy[zi, k] = send(blocks[zi, 0], xpart, cols[k], to(dy=k))

    def y_across(zi):
        for k in (1, 3):
            yy[zi, k] = send(blocks[zi, 0], yrows, cols[k], to(dy=k))

    def received(*copies):
        for copy in copies:
            copy.wait_recv()

    for k in KS:
        xz[k] = send(own, xpart, every, to(dz=k))
    x_across(0)
    for k in (1, 3):
        zy[k] = send(own, zrows, cols[k], to(dy=k))
    zyz[1] = send(own, zyrows, every, to(dz=1))
    share(0, 0, (0, height))
    for zi in KS:
        received(xz[zi])
        x_across(zi)
    y_across(0)
    received(xy[0, 1], xy[0, 3])
    x_down(0, 1)
    received(zy[1], zy[3])
    zz[1] = send(blocks[0, 1], zrows, every, to(dz=1))
    share(0, 1, zrows)
    for k in (3, 2):
        zyz[k] = send(own, zyrows, every, to(dz=k))
        zz[k] = send(blocks[0, 1], zrows, every, to(dz=k))
    for zi in KS:
        x_down(zi, 0)
        received(xy[zi, 1], xy[zi, 3])
        x_down(zi, 1)

    count = tokens.shape[0]
    per_sample = count // factor.shape[0]

    def normalize(step, _):
        at = pl.ds(pl.multiple_of(step * 16, 16), 16)
        value = tokens[at, :].astype(jnp.float32)
        centre = value - jnp.mean(value, axis=1, keepdims=True)
        inverse = lax.rsqrt(jnp.mean(centre * centre, axis=1, keepdims=True) + epsilon)
        sample = pl.ds(step * 16 // per_sample, 1)
        moved[at, :] = (centre * inverse * factor[sample, :] + shift[sample, :]).astype(
            jnp.bfloat16
        )
        return 0

    lax.fori_loop(0, count // 16, normalize, 0)

    low = z % 2
    plan = []
    for zi, tiles in ((0, NEAR), (1, FAR), (3, NEAR), (2, FAR)):
        high = flip(z, zi) % 2
        first = 19 * (flip(z, zi) // 2) + high * (19 - tiles)
        plan.append((zi, tiles * TILE, pl.multiple_of(first * TILE, TILE)))

    def fetch(n):
        zi, size, at = plan[n]
        copy = pltpu.make_async_copy(
            cotangent.at[:, pl.ds(at, size)],
            upstream.at[n % 2, :, pl.ds(0, size)],
            up_sem.at[n % 2],
        )
        copy.start()
        return copy

    fetched = [fetch(0), fetch(1)]
    stores = []
    saved = []

    def window(n):
        zi, size, at = plan[n]
        slot = n % 2
        fetched[n].wait()
        if n >= 2:
            for copy in stores[n - 2]:
                copy.wait()

        def piece(begin, width):
            values = whole[pl.ds(pl.multiple_of(at + begin, TILE), width), :]
            preact = lax.dot_general(
                moved[...], values, (((1,), (1,)), ((), ())),
                preferred_element_type=jnp.float32,
            )
            gelu_value, derivative = gelu_slope(preact)
            columns = pl.ds(begin, width)
            hidden_part[slot, :, columns] = gelu_value.astype(jnp.bfloat16)
            grad = (upstream[slot, :, columns].astype(jnp.float32) * derivative).astype(
                jnp.bfloat16
            )
            gradient_part[slot, :, columns] = grad
            rows_part[slot, columns, :] = grad.T

        def step(i, _):
            piece(pl.multiple_of(i * CHUNK, CHUNK), CHUNK)
            return 0

        lax.fori_loop(0, size // CHUNK, step, 0)
        if size % CHUNK:
            piece(size - size % CHUNK, size % CHUNK)
        target = pl.ds(at, size)
        copies = [
            pltpu.make_async_copy(
                hidden_part.at[slot, :, pl.ds(0, size)], hidden.at[:, target], out_sem.at[0, slot]
            ),
            pltpu.make_async_copy(
                gradient_part.at[slot, :, pl.ds(0, size)], gradient.at[:, target],
                out_sem.at[1, slot],
            ),
            pltpu.make_async_copy(
                rows_part.at[slot, pl.ds(0, size), :], gradient_rows.at[target, :],
                out_sem.at[2, slot],
            ),
        ]
        for copy in copies:
            copy.start()
        stores.append(copies)
        if n + 2 < len(plan):
            fetched.append(fetch(n + 2))

    def land(zi):
        if zi:
            received(zz[zi])
            share(zi, 1, zrows)
        received(yy[zi, 1], yy[zi, 3])
        share(zi, 1, yrows)
        for yi in (0, 1):
            for k in KS if zi or yi else ():
                received(xx[zi, yi, k])
                share(zi, yi, (GX_PART * flip(x, k), GX_PART))
        received(*shared[zi])
        landed = within(4 * flip(z, zi), (0, 4 * height))
        copy = pltpu.make_async_copy(
            whole.at[landed, :], whole_out.at[landed, :], whole_sem.at[zi]
        )
        copy.start()
        saved.append(copy)

    def relay(zi):
        received(zyz[zi])
        y_across(zi)
        share(zi, 0, zyrows)

    keep.wait()
    relay(1)
    land(0)
    window(0)
    relay(3)
    land(1)
    window(1)
    land(3)
    relay(2)
    window(2)
    land(2)
    window(3)
    for copies in stores[2:]:
        for copy in copies:
            copy.wait()
    for copy in saved:
        copy.wait()
    for copy in started:
        copy.wait_send()


def forward_blocks(mine, tokens, shift, factor, cotangent):
    rows, features = mine.shape
    count, units = cotangent.shape
    copies, widest = 120, FAR * TILE
    bf16 = jnp.bfloat16
    vmem = pl.BlockSpec(memory_space=pltpu.VMEM)
    anywhere = pl.BlockSpec(memory_space=pl.ANY)
    return pl.pallas_call(
        forward_kernel,
        out_shape=(
            jax.ShapeDtypeStruct((16 * rows, features), bf16),
            jax.ShapeDtypeStruct((count, units), bf16),
            jax.ShapeDtypeStruct((count, units), bf16),
            jax.ShapeDtypeStruct((units, count), bf16),
            jax.ShapeDtypeStruct((count, features), bf16),
        ),
        in_specs=[vmem, vmem, vmem, vmem, anywhere],
        out_specs=(anywhere, anywhere, anywhere, anywhere, vmem),
        scratch_shapes=[
            pltpu.VMEM((16 * rows, features), bf16),
            pltpu.VMEM((2, count, widest), bf16),
            pltpu.VMEM((2, count, widest), bf16),
            pltpu.VMEM((2, count, widest), bf16),
            pltpu.VMEM((2, widest, count), bf16),
            pltpu.SemaphoreType.DMA(()),
            pltpu.SemaphoreType.DMA((copies,)),
            pltpu.SemaphoreType.DMA((copies,)),
            pltpu.SemaphoreType.DMA((2,)),
            pltpu.SemaphoreType.DMA((3, 2)),
            pltpu.SemaphoreType.DMA((4,)),
        ],
        compiler_params=pltpu.CompilerParams(
            collective_id=1, has_side_effects=True, vmem_limit_bytes=60 << 20
        ),
        name="forward_blocks",
    )(mine, tokens, shift, factor, cotangent)


def per_device(tokens, timesteps, table, weight_values, weight_scales, cotangent):
    shift, factor = pick(timesteps, table)
    weight, hidden, grad_pre, gradient_rows, moved = forward_blocks(
        dequantize(weight_values, weight_scales), tokens, shift, factor, cotangent
    )
    grad_weight, grad_tokens = reduce_blocks(
        gradient_rows, grad_pre, moved, weight, tokens, factor
    )
    return (hidden, grad_weight, grad_tokens)


def solution(mesh):
    placed = (
        P(("replica", "shard"), None),
        P(("replica", "shard")),
        P(),
        P("shard", None),
        P("shard", None),
        P(("replica", "shard"), None),
    )
    return jax.shard_map(
        per_device,
        mesh=mesh,
        in_specs=placed,
        out_specs=(P(("replica", "shard"), None), P("shard", None), P(("replica", "shard"), None)),
        check_vma=False,
    )
```

```python
import jax
import jax.numpy as jnp
from jax import lax
from jax.experimental import pallas as pl
from jax.experimental.pallas import tpu as pltpu
from jax.sharding import PartitionSpec as P

root_two_over_pi = 0.7978845608028654
cubic_coef = 0.044715
epsilon = 1e-06


def gelu_slope(preact):
    inner_term = root_two_over_pi * (preact + cubic_coef * preact * preact * preact)
    tangent = jnp.tanh(inner_term)
    gelu_value = 0.5 * preact * (1.0 + tangent)
    derivative = 0.5 * (1.0 + tangent) + 0.5 * preact * (
        1.0 - tangent * tangent
    ) * root_two_over_pi * (1.0 + 3.0 * cubic_coef * preact * preact)
    return (gelu_value, derivative)


def dequantize(weight_values, weight_scales):
    row_count, features = weight_values.shape
    blocks = weight_scales.shape[1]
    expanded = (
        weight_values.astype(jnp.float32).reshape(row_count, blocks, features // blocks)
        * weight_scales.astype(jnp.float32)[:, :, None]
    )
    return expanded.reshape(row_count, features).astype(jnp.bfloat16)


def pick(timesteps, table):
    step_count, _, features = table.shape
    onehot = (timesteps[:, None] == jnp.arange(step_count, dtype=jnp.int32)[None, :]).astype(
        jnp.float32
    )
    picked = jnp.dot(
        onehot, table.reshape(step_count, 2 * features), precision=lax.Precision.HIGHEST
    )
    return picked[:, :features], 1.0 + picked[:, features:]


MESH = pl.DeviceIdType.MESH
KS = (1, 3, 2)
Z_ROWS, X_ROWS, Y_ROWS = 96, 96, 112
X_AT, Y_AT = Z_ROWS, Z_ROWS + X_ROWS
OWN_ROWS = Z_ROWS + X_ROWS + Y_ROWS
WINDOWS = ((0, 1024), (1024, 1024), (2048, 1024), (3072, 1024), (4096, 768))


def flip(value, k):
    low, high = value % 2, value // 2
    if k & 1:
        low = 1 - low
    if k & 2:
        high = 1 - high
    return 2 * high + low


def place():
    replica, shard = lax.axis_index("replica"), lax.axis_index("shard")
    return (replica // 2, 2 * (replica % 2) + (shard // 2) % 2, shard // 4, shard % 2)


def device_at(x, y, z, core):
    return (2 * x + y // 2, (2 * z + y % 2) * 2 + core)


def quarter(x):
    return pl.multiple_of(jnp.minimum(512 * x, 1408), 128)


def half(y):
    return pl.multiple_of(896 * (y // 2), 128)


def part(v):
    return pl.multiple_of(256 * v, 128)


def add_rows(rows, store, loads):
    def body(step, _):
        at = pl.ds(pl.multiple_of(step * 16, 16), 16)
        total = loads[0](at).astype(jnp.float32)
        for load in loads[1:]:
            total = total + load(at).astype(jnp.float32)
        store(at, total)
        return 0

    lax.fori_loop(0, rows // 16, body, 0)


def reduce_kernel(
    gradient_rows, gradient, moved, weight, tokens, factor, out, grad_tokens, grad_moved, own, operand, tokens_all,
    weight_parts, gradient_parts, zr1, zr2, zr3, xr1, xr2, xr3, yr1, yr2, yr3,
    zb, zc, xb, xc, yb, yc, pieces, local_sem, core_sem, part_sem, s1, r1, s2, r2, s3, r3, s4, r4,
):
    x, y, z, core = place()

    def to(dx=0, dy=0, dz=0, dc=0):
        return device_at(flip(x, dx), flip(y, dy), flip(z, dz), 1 - core if dc else core)

    peers = [to(dc=1)]
    peers += [to(dx=k) for k in KS] + [to(dy=k) for k in KS] + [to(dz=k) for k in KS]
    barrier = pltpu.get_barrier_semaphore()
    for peer in peers:
        pl.semaphore_signal(barrier, inc=1, device_id=peer, device_id_type=MESH)
    pl.semaphore_wait(barrier, len(peers))

    started = []

    def send(src, dst, send_sem, recv_sem, peer):
        copy = pltpu.make_async_remote_copy(
            src_ref=src, dst_ref=dst, send_sem=send_sem, recv_sem=recv_sem,
            device_id=peer, device_id_type=MESH,
        )
        copy.start()
        started.append(copy)
        return copy

    def fetch(w):
        at, size = WINDOWS[w]
        return [
            pltpu.make_async_copy(
                weight.at[pl.ds(at, size), :],
                weight_parts.at[w % 2, pl.ds(0, size), :],
                part_sem.at[0, w % 2],
            ),
            pltpu.make_async_copy(
                gradient.at[:, pl.ds(at, size)],
                gradient_parts.at[w % 2, :, pl.ds(0, size)],
                part_sem.at[1, w % 2],
            ),
        ]

    count = moved.shape[0]
    lanes = pl.ds(pl.multiple_of(core * count, 128), count)
    mine_moved = pltpu.make_async_copy(moved, tokens_all.at[lanes, :], local_sem.at[8])
    mine_moved.start()
    their_moved = send(
        moved, tokens_all.at[lanes, :], core_sem.at[0, 8], core_sem.at[1, 8], to(dc=1)
    )
    swaps = {}
    order = [(zi, yi) for zi in (1, 3, 2, 0) for yi in (1, 0)]
    for n, (zi, yi) in enumerate(order):
        block = 2 * flip(z, zi) + flip(y, yi) % 2
        mine = pltpu.make_async_copy(
            gradient_rows.at[2 * block + core], operand.at[zi, yi, :, lanes], local_sem.at[n]
        )
        mine.start()
        theirs = send(
            gradient_rows.at[2 * block + 1 - core], operand.at[zi, yi, :, lanes],
            core_sem.at[0, n], core_sem.at[1, n], to(dc=1),
        )
        swaps[zi, yi] = (mine, theirs)
    windows = [fetch(0), fetch(1)]
    for pair in windows:
        for copy in pair:
            copy.start()
    mine_moved.wait()
    their_moved.wait_recv()

    first = {"z": [], "x": [], "y": []}
    for zi, yi in order:
        if yi:
            for each in (1, 0):
                mine, theirs = swaps[zi, each]
                mine.wait()
                theirs.wait_recv()
            rows = operand[zi].reshape(2 * OWN_ROWS, 2 * count)
            for at, size in ((0, 1024), (1024, 896)):
                term = jnp.dot(
                    rows, tokens_all[:, at : at + size], preferred_element_type=jnp.float32
                )
                own[zi, :, :, at : at + size] = term.astype(jnp.bfloat16).reshape(
                    2, OWN_ROWS, size
                )
        if zi:
            n = (zi - 1) * 2 + yi
            first["z"].append(send(
                own.at[zi, yi, pl.ds(0, Z_ROWS), :], zr1.at[zi - 1, yi],
                s1.at[n], r1.at[n], to(dz=zi),
            ))
        for k in KS:
            n = 6 + (zi * 2 + yi) * 3 + k - 1
            first["x"].append(send(
                own.at[zi, yi, pl.ds(X_AT, X_ROWS), pl.ds(quarter(flip(x, k)), 512)],
                xr1.at[k - 1, zi, yi], s1.at[n], r1.at[n], to(dx=k),
            ))
        for k in (1, 3) if yi else (2,):
            n = 30 + zi * 3 + k - 1
            first["y"].append(send(
                own.at[zi, yi, pl.ds(Y_AT, Y_ROWS), pl.ds(half(flip(y, k)), 1024)],
                yr1.at[k - 1, zi], s1.at[n], r1.at[n], to(dy=k),
            ))

    for w in range(len(WINDOWS)):
        for copy in windows[w]:
            copy.wait()
        size = WINDOWS[w][1]
        for at, width in ((0, 1024), (1024, 896)):
            term = jnp.dot(
                gradient_parts[w % 2, :, 0:size],
                weight_parts[w % 2, 0:size, at : at + width],
                preferred_element_type=jnp.float32,
            )
            columns = slice(at, at + width)
            grad_moved[:, columns] = term if w == 0 else grad_moved[:, columns] + term
        if w + 2 < len(WINDOWS):
            windows.append(fetch(w + 2))
            for copy in windows[w + 2]:
                copy.start()

    def store_to(ref):
        def store(at, total):
            ref[at, :] = total.astype(jnp.bfloat16)

        return store

    def shifted(ref, base, columns):
        return lambda at: ref[pl.ds(base + at.start, at.size), columns]

    def plain(ref):
        return lambda at: ref[at, :]

    second = {"z": [], "x": [], "y": []}
    for copy in first["z"]:
        copy.wait_recv()
    for yi in (0, 1):
        add_rows(
            Z_ROWS, store_to(zb.at[yi]),
            [plain(own.at[0, yi])] + [plain(zr1.at[k - 1, yi]) for k in KS],
        )
    for k in KS:
        second["z"].append(send(
            zb.at[:, :, pl.ds(quarter(flip(x, k)), 512)], zr2.at[k - 1],
            s2.at[k - 1], r2.at[k - 1], to(dx=k),
        ))
    for copy in first["x"]:
        copy.wait_recv()
    for yi in (1, 0):
        for zi in range(4):
            columns = pl.ds(quarter(x), 512)
            add_rows(
                X_ROWS, store_to(xb.at[zi, yi]),
                [shifted(own.at[zi, yi], X_AT, columns)]
                + [plain(xr1.at[k - 1, zi, yi]) for k in KS],
            )
        for k in (1, 3) if yi else (2,):
            second["x"].append(send(
                xb.at[:, yi, :, pl.ds(part(flip(y, k) // 2), 256)], xr2.at[k - 1],
                s2.at[5 + k], r2.at[5 + k], to(dy=k),
            ))
    for copy in first["y"]:
        copy.wait_recv()
    for zi in (1, 3, 2, 0):
        columns = pl.ds(half(y), 1024)
        add_rows(
            Y_ROWS, store_to(yb.at[zi]),
            [shifted(own.at[zi, 0], Y_AT, columns)] + [plain(yr1.at[k - 1, zi]) for k in KS],
        )
        if zi:
            second["y"].append(send(
                yb.at[zi], yr2.at[zi - 1], s2.at[2 + zi], r2.at[2 + zi], to(dz=zi)
            ))

    per_sample = count // factor.shape[0]

    def finish(step, _):
        at = pl.ds(pl.multiple_of(step * 16, 16), 16)
        value = tokens[at, :].astype(jnp.float32)
        centre = value - jnp.mean(value, axis=1, keepdims=True)
        inverse = lax.rsqrt(jnp.mean(centre * centre, axis=1, keepdims=True) + epsilon)
        normed = centre * inverse
        scaled_grad = grad_moved[at, :] * factor[pl.ds(step * 16 // per_sample, 1), :]
        mean_grad = jnp.mean(scaled_grad, axis=1, keepdims=True)
        mean_prod = jnp.mean(scaled_grad * normed, axis=1, keepdims=True)
        result = inverse * (scaled_grad - mean_grad - normed * mean_prod)
        grad_tokens[at, :] = result.astype(jnp.bfloat16)
        return 0

    lax.fori_loop(0, count // 16, finish, 0)

    third = {"z": [], "x": [], "y": []}
    for copy in second["z"]:
        copy.wait_recv()
    for yi in (1, 0):
        columns = pl.ds(quarter(x), 512)
        add_rows(
            Z_ROWS, store_to(zc.at[yi]),
            [shifted(zb.at[yi], 0, columns)] + [plain(zr2.at[k - 1, yi]) for k in KS],
        )
        for k in (1, 3) if yi else (2,):
            third["z"].append(send(
                zc.at[yi, :, pl.ds(part(flip(y, k) // 2), 256)], zr3.at[k - 1],
                s3.at[k - 1], r3.at[k - 1], to(dy=k),
            ))
    for copy in second["y"]:
        copy.wait_recv()
    add_rows(Y_ROWS, store_to(yc), [plain(yb.at[0])] + [plain(yr2.at[k - 1]) for k in KS])
    for k in KS:
        third["y"].append(send(
            yc.at[:, pl.ds(part(flip(x, k)), 256)], yr3.at[k - 1],
            s3.at[2 + k], r3.at[2 + k], to(dx=k),
        ))
    for copy in second["x"]:
        copy.wait_recv()
    for zi in (1, 3, 2, 0):
        columns = pl.ds(part(y // 2), 256)
        add_rows(
            X_ROWS, store_to(xc.at[zi]),
            [shifted(xb.at[zi, 0], 0, columns)] + [plain(xr2.at[k - 1, zi]) for k in KS],
        )
        if zi:
            third["x"].append(send(
                xc.at[zi], xr3.at[zi - 1], s3.at[5 + zi], r3.at[5 + zi], to(dz=zi)
            ))

    def store_piece(base):
        def store(at, total):
            pieces[0, pl.ds(base + at.start, at.size), :] = total.astype(jnp.bfloat16)

        return store

    for copy in third["z"]:
        copy.wait_recv()
    columns = pl.ds(part(y // 2), 256)
    add_rows(
        Z_ROWS, store_piece(0),
        [shifted(zc.at[0], 0, columns)] + [plain(zr3.at[k - 1]) for k in KS],
    )
    for copy in third["y"]:
        copy.wait_recv()
    own_columns = pl.ds(part(x), 256)
    add_rows(
        Y_ROWS, store_piece(Y_AT),
        [shifted(yc, 0, own_columns)] + [plain(yr3.at[k - 1]) for k in KS],
    )
    for copy in third["x"]:
        copy.wait_recv()
    add_rows(
        X_ROWS, store_piece(X_AT), [plain(xc.at[0])] + [plain(xr3.at[k - 1]) for k in KS]
    )

    def hand(source, slot, peer):
        return send(
            pieces.at[source], pieces.at[slot], s4.at[slot - 1], r4.at[slot - 1], peer
        )

    along = {k: hand(0, 2 * k, to(dx=k)) for k in KS}
    across = [hand(0, 1, to(dy=2))]
    for k in KS:
        along[k].wait_recv()
        across.append(hand(2 * k, 2 * k + 1, to(dy=2)))
    for copy in across:
        copy.wait_recv()
    for px in range(4):
        for ph in range(2):
            lows = (px % 2 + x % 2) % 2
            highs = (px // 2 + x // 2) % 2
            slot = 2 * (2 * highs + lows) + (ph + y // 2) % 2
            at = min(512 * px, 1408) + 256 * ph
            out[0:Y_AT, at : at + 256] = pieces[slot, 0:Y_AT, :].astype(jnp.float32)
    for ph in range(2):
        for px in range(4):
            lows = (px % 2 + x % 2) % 2
            highs = (px // 2 + x // 2) % 2
            slot = 2 * (2 * highs + lows) + (ph + y // 2) % 2
            at = 896 * ph + 256 * px
            out[Y_AT:OWN_ROWS, at : at + 256] = pieces[slot, Y_AT:OWN_ROWS, :].astype(jnp.float32)
    for copy in started:
        copy.wait_send()


def reduce_blocks(gradient_rows, grad_pre, moved, weight, tokens, factor):
    count, features = moved.shape
    bf16 = jnp.bfloat16
    shapes = [
        (4, 2, OWN_ROWS, features), (4, 2, OWN_ROWS, 2 * count), (2 * count, features),
        (2, 1024, features), (2, count, 1024),
        (3, 2, Z_ROWS, features), (3, 2, Z_ROWS, 512), (3, Z_ROWS, 256),
        (3, 4, 2, X_ROWS, 512), (3, 4, X_ROWS, 256), (3, X_ROWS, 256),
        (3, 4, Y_ROWS, 1024), (3, Y_ROWS, 1024), (3, Y_ROWS, 256),
        (2, Z_ROWS, features), (2, Z_ROWS, 512),
        (4, 2, X_ROWS, 512), (4, X_ROWS, 256),
        (4, Y_ROWS, 1024), (Y_ROWS, 1024),
        (8, OWN_ROWS, 256),
    ]
    sems = [(9,), (2, 9), (2, 2), (42,), (42,), (9,), (9,), (9,), (9,), (7,), (7,)]
    return pl.pallas_call(
        reduce_kernel,
        out_shape=(
            jax.ShapeDtypeStruct((OWN_ROWS, features), jnp.float32),
            jax.ShapeDtypeStruct((count, features), bf16),
        ),
        in_specs=[pl.BlockSpec(memory_space=pl.ANY)] * 4
        + [pl.BlockSpec(memory_space=pltpu.VMEM)] * 2,
        out_specs=[pl.BlockSpec(memory_space=pltpu.VMEM)] * 2,
        scratch_shapes=[pltpu.VMEM((count, features), jnp.float32)]
        + [pltpu.VMEM(shape, bf16) for shape in shapes]
        + [pltpu.SemaphoreType.DMA(shape) for shape in sems],
        compiler_params=pltpu.CompilerParams(
            collective_id=0, has_side_effects=True, vmem_limit_bytes=60 << 20
        ),
        name="reduce_blocks",
    )(gradient_rows.reshape(-1, OWN_ROWS, count), grad_pre, moved, weight, tokens, factor)


GX_ROWS, GZ_ROWS, GY_ROWS = 128, 32, 144
GX_PART = GX_ROWS // 4
GY_AT = GX_ROWS + GZ_ROWS
HALVES = {1: (0, 1024), 3: (1024, 896)}
TILE = 128
NEAR, FAR = 9, 10
CHUNK = 256


def forward_kernel(
    mine, tokens, shift, factor, cotangent,
    whole_out, hidden, gradient, gradient_rows, moved,
    whole, upstream, hidden_part, gradient_part, rows_part,
    own_sem, ss, rs, up_sem, out_sem, whole_sem,
):
    x, y, z, core = place()

    def to(dx=0, dy=0, dz=0, dc=0):
        return device_at(flip(x, dx), flip(y, dy), flip(z, dz), 1 - core if dc else core)

    peers = [to(dc=1)]
    peers += [to(dx=k) for k in KS] + [to(dy=k) for k in (1, 3)] + [to(dz=k) for k in KS]
    barrier = pltpu.get_barrier_semaphore()
    for peer in peers:
        pl.semaphore_signal(barrier, inc=1, device_id=peer, device_id_type=MESH)
    pl.semaphore_wait(barrier, len(peers))

    started = []

    def block_of(zi, yi):
        return 2 * (2 * flip(z, zi) + flip(y, yi) % 2) + core

    blocks = {(zi, yi): block_of(zi, yi) for zi in range(4) for yi in (0, 1)}
    own = blocks[0, 0]
    height = mine.shape[0]

    def within(block, rows):
        return pl.ds(pl.multiple_of(height * block + rows[0], 16), rows[1])

    def send(block, rows, columns, peer):
        n = len(started)
        if block is own:
            source = mine.at[pl.ds(*rows), columns]
        else:
            source = whole.at[within(block, rows), columns]
        copy = pltpu.make_async_remote_copy(
            src_ref=source,
            dst_ref=whole.at[within(block, rows), columns],
            send_sem=ss.at[n], recv_sem=rs.at[n],
            device_id=peer, device_id_type=MESH,
        )
        copy.start()
        started.append(copy)
        return copy

    every = slice(None)
    keep = pltpu.make_async_copy(mine, whole.at[within(own, (0, height)), :], own_sem)
    keep.start()
    shared = {0: [], 1: [], 3: [], 2: []}

    def share(zi, yi, rows):
        shared[zi].append(send(blocks[zi, yi], rows, every, to(dc=1)))

    xpart = (GX_PART * x, GX_PART)
    zrows, yrows = (GX_ROWS, GZ_ROWS), (GY_AT, GY_ROWS)
    zyrows = (GX_ROWS, GZ_ROWS + GY_ROWS)
    cols = {k: pl.ds(*HALVES[k]) for k in HALVES}
    xz, xy, xx, zyz, yy, zy, zz = {}, {}, {}, {}, {}, {}, {}

    def x_down(zi, yi):
        for k in KS:
            xx[zi, yi, k] = send(blocks[zi, yi], xpart, every, to(dx=k))
        share(zi, yi, xpart)

    def x_across(zi):
        for k in (1, 3):
            xy[zi, k] = send(blocks[zi, 0], xpart, cols[k], to(dy=k))

    def y_across(zi):
        for k in (1, 3):
            yy[zi, k] = send(blocks[zi, 0], yrows, cols[k], to(dy=k))

    def received(*copies):
        for copy in copies:
            copy.wait_recv()

    for k in KS:
        xz[k] = send(own, xpart, every, to(dz=k))
    x_across(0)
    for k in (1, 3):
        zy[k] = send(own, zrows, cols[k], to(dy=k))
    zyz[1] = send(own, zyrows, every, to(dz=1))
    share(0, 0, (0, height))
    for zi in KS:
        received(xz[zi])
        x_across(zi)
    y_across(0)
    received(xy[0, 1], xy[0, 3])
    x_down(0, 1)
    received(zy[1], zy[3])
    zz[1] = send(blocks[0, 1], zrows, every, to(dz=1))
    share(0, 1, zrows)
    for k in (3, 2):
        zyz[k] = send(own, zyrows, every, to(dz=k))
        zz[k] = send(blocks[0, 1], zrows, every, to(dz=k))
    for zi in KS:
        x_down(zi, 0)
        received(xy[zi, 1], xy[zi, 3])
        x_down(zi, 1)

    count = tokens.shape[0]
    per_sample = count // factor.shape[0]

    def normalize(step, _):
        at = pl.ds(pl.multiple_of(step * 16, 16), 16)
        value = tokens[at, :].astype(jnp.float32)
        centre = value - jnp.mean(value, axis=1, keepdims=True)
        inverse = lax.rsqrt(jnp.mean(centre * centre, axis=1, keepdims=True) + epsilon)
        sample = pl.ds(step * 16 // per_sample, 1)
        moved[at, :] = (centre * inverse * factor[sample, :] + shift[sample, :]).astype(
            jnp.bfloat16
        )
        return 0

    lax.fori_loop(0, count // 16, normalize, 0)

    low = z % 2
    plan = []
    for zi, tiles in ((0, NEAR), (1, FAR), (3, NEAR), (2, FAR)):
        high = flip(z, zi) % 2
        first = 19 * (flip(z, zi) // 2) + high * (19 - tiles)
        plan.append((zi, tiles * TILE, pl.multiple_of(first * TILE, TILE)))

    def fetch(n):
        zi, size, at = plan[n]
        copy = pltpu.make_async_copy(
            cotangent.at[:, pl.ds(at, size)],
            upstream.at[n % 2, :, pl.ds(0, size)],
            up_sem.at[n % 2],
        )
        copy.start()
        return copy

    fetched = [fetch(0), fetch(1)]
    stores = []
    saved = []

    def window(n):
        zi, size, at = plan[n]
        slot = n % 2
        fetched[n].wait()
        if n >= 2:
            for copy in stores[n - 2]:
                copy.wait()

        def piece(begin, width):
            values = whole[pl.ds(pl.multiple_of(at + begin, TILE), width), :]
            preact = lax.dot_general(
                moved[...], values, (((1,), (1,)), ((), ())),
                preferred_element_type=jnp.float32,
            )
            gelu_value, derivative = gelu_slope(preact)
            columns = pl.ds(begin, width)
            hidden_part[slot, :, columns] = gelu_value.astype(jnp.bfloat16)
            grad = (upstream[slot, :, columns].astype(jnp.float32) * derivative).astype(
                jnp.bfloat16
            )
            gradient_part[slot, :, columns] = grad
            rows_part[slot, columns, :] = grad.T

        def step(i, _):
            piece(pl.multiple_of(i * CHUNK, CHUNK), CHUNK)
            return 0

        lax.fori_loop(0, size // CHUNK, step, 0)
        if size % CHUNK:
            piece(size - size % CHUNK, size % CHUNK)
        target = pl.ds(at, size)
        copies = [
            pltpu.make_async_copy(
                hidden_part.at[slot, :, pl.ds(0, size)], hidden.at[:, target], out_sem.at[0, slot]
            ),
            pltpu.make_async_copy(
                gradient_part.at[slot, :, pl.ds(0, size)], gradient.at[:, target],
                out_sem.at[1, slot],
            ),
            pltpu.make_async_copy(
                rows_part.at[slot, pl.ds(0, size), :], gradient_rows.at[target, :],
                out_sem.at[2, slot],
            ),
        ]
        for copy in copies:
            copy.start()
        stores.append(copies)
        if n + 2 < len(plan):
            fetched.append(fetch(n + 2))

    def land(zi):
        if zi:
            received(zz[zi])
            share(zi, 1, zrows)
        received(yy[zi, 1], yy[zi, 3])
        share(zi, 1, yrows)
        for yi in (0, 1):
            for k in KS if zi or yi else ():
                received(xx[zi, yi, k])
                share(zi, yi, (GX_PART * flip(x, k), GX_PART))
        received(*shared[zi])
        landed = within(4 * flip(z, zi), (0, 4 * height))
        copy = pltpu.make_async_copy(
            whole.at[landed, :], whole_out.at[landed, :], whole_sem.at[zi]
        )
        copy.start()
        saved.append(copy)

    def relay(zi):
        received(zyz[zi])
        y_across(zi)
        share(zi, 0, zyrows)

    keep.wait()
    relay(1)
    land(0)
    window(0)
    relay(3)
    land(1)
    window(1)
    land(3)
    relay(2)
    window(2)
    land(2)
    window(3)
    for copies in stores[2:]:
        for copy in copies:
            copy.wait()
    for copy in saved:
        copy.wait()
    for copy in started:
        copy.wait_send()


def forward_blocks(mine, tokens, shift, factor, cotangent):
    rows, features = mine.shape
    count, units = cotangent.shape
    copies, widest = 120, FAR * TILE
    bf16 = jnp.bfloat16
    vmem = pl.BlockSpec(memory_space=pltpu.VMEM)
    anywhere = pl.BlockSpec(memory_space=pl.ANY)
    return pl.pallas_call(
        forward_kernel,
        out_shape=(
            jax.ShapeDtypeStruct((16 * rows, features), bf16),
            jax.ShapeDtypeStruct((count, units), bf16),
            jax.ShapeDtypeStruct((count, units), bf16),
            jax.ShapeDtypeStruct((units, count), bf16),
            jax.ShapeDtypeStruct((count, features), bf16),
        ),
        in_specs=[vmem, vmem, vmem, vmem, anywhere],
        out_specs=(anywhere, anywhere, anywhere, anywhere, vmem),
        scratch_shapes=[
            pltpu.VMEM((16 * rows, features), bf16),
            pltpu.VMEM((2, count, widest), bf16),
            pltpu.VMEM((2, count, widest), bf16),
            pltpu.VMEM((2, count, widest), bf16),
            pltpu.VMEM((2, widest, count), bf16),
            pltpu.SemaphoreType.DMA(()),
            pltpu.SemaphoreType.DMA((copies,)),
            pltpu.SemaphoreType.DMA((copies,)),
            pltpu.SemaphoreType.DMA((2,)),
            pltpu.SemaphoreType.DMA((3, 2)),
            pltpu.SemaphoreType.DMA((4,)),
        ],
        compiler_params=pltpu.CompilerParams(
            collective_id=1, has_side_effects=True, vmem_limit_bytes=60 << 20
        ),
        name="forward_blocks",
    )(mine, tokens, shift, factor, cotangent)


def per_device(tokens, timesteps, table, weight_values, weight_scales, cotangent):
    shift, factor = pick(timesteps, table)
    weight, hidden, grad_pre, gradient_rows, moved = forward_blocks(
        dequantize(weight_values, weight_scales), tokens, shift, factor, cotangent
    )
    grad_weight, grad_tokens = reduce_blocks(
        gradient_rows, grad_pre, moved, weight, tokens, factor
    )
    return (hidden, grad_weight, grad_tokens)


def solution(mesh):
    placed = (
        P(("replica", "shard"), None),
        P(("replica", "shard")),
        P(),
        P("shard", None),
        P("shard", None),
        P(("replica", "shard"), None),
    )
    return jax.shard_map(
        per_device,
        mesh=mesh,
        in_specs=placed,
        out_specs=(P(("replica", "shard"), None), P("shard", None), P(("replica", "shard"), None)),
        check_vma=False,
    )
```
